128 devices in a mesh: gx: 16 (over z, x), gy: 8 (over y, core).
Axes of the slice: x: 4, y: 4, z: 4, core: 2. Of those that a mesh axis runs over, the one named last changes fastest.
Arguments:
- length_scale: float32 [128, 512, 128], P('gx', 'gy'), may hold values from 0.35 to 1
- innovation: float32 [262144], P(('gx', 'gy')), may hold values from -6 to 6
- observed_precision: float32 [262144], P(('gx', 'gy')), may hold values from 0.25 to 4
- profile_weight: float32 [262144, 128], P(('gx', 'gy')), may hold values from -0.5 to 0.5
- stencil_weight: float32 [4, 262144], P(None, ('gx', 'gy')), may hold values from 0.05 to 0.45
- send_rows: int32 [128, 128, 16], P(('gx', 'gy')), may hold values from 0 to 511, as said below
- stencil_rows: int32 [4, 262144], P(None, ('gx', 'gy')), may hold values from 0 to 2047, as said below
- obs_count: int32 [128], P(('gx', 'gy')), may hold values from 256 to 2048
Outputs:
- control: float32 [128, 512, 128], P('gx', 'gy')
- increment: float32 [128, 512, 128], P('gx', 'gy')
The draws below stay inside these ranges and needn't reach their ends.
Inputs may be any that keep to these rules, and one draw needn't show every extreme that they name: `send_rows`: every entry is a column of the source's tile. Slots of a pair beyond the pair's used count hold 0 and are named by no stencil entry; each pair uses between 4 and 16 slots, one source uses all slots toward every owner, and one owner receives full slots from every source. `stencil_rows`: each entry names a used slot of the pair from its source to the observation's owner, also for slots that are not live.
All inputs are finite; a program needn't handle non-finite values.
Results may differ from the reference program's by a relative error of at most 0.007.
Values sent between devices are 32-bit elements; how exact they have to be, the bound alone decides.
No kernel may reach another device: no remote copies, remote signals or barrier semaphores. Data moves between devices by JAX's collectives and lax.ppermute only.
A program may use at most 64 MiB of HBM per device.

```python
import math
import jax
import jax.numpy as jnp
from jax import lax

CX = 8
CY = 64
LEV = 128
OBS_DEV = 2048
SLOTS = 16
PASSES = 4
ITERS = 2
OWNERS = 128
NX = 128
NY = 512
OBS = 262144
N_GX = 16
N_GY = 8


def pair_counts(key):
    folded = jax.random.fold_in(key, 11)
    counts = jax.random.randint(jax.random.fold_in(folded, 1), (OWNERS, OWNERS), SLOTS // 4, SLOTS + 1)
    sender = jax.random.randint(jax.random.fold_in(folded, 2), (), 0, OWNERS)
    receiver = jax.random.randint(jax.random.fold_in(folded, 3), (), 0, OWNERS)
    counts = counts.at[sender, :].set(SLOTS)
    counts = counts.at[:, receiver].set(SLOTS)
    return (counts, receiver)


def draw_send_rows(key, part):
    counts, receiver = pair_counts(key)
    columns = jax.random.randint(jax.random.fold_in(key, 12), (OWNERS, OWNERS, SLOTS), 0, CX * CY)
    in_use = jnp.arange(SLOTS, dtype=jnp.int32)[None, None, :] < counts[:, :, None]
    return jnp.where(in_use, columns, 0).astype(jnp.int32)


def draw_stencil_rows(key, part):
    counts, receiver = pair_counts(key)
    source = jax.random.randint(jax.random.fold_in(key, 13), (4, OWNERS * OBS_DEV), 0, OWNERS)
    target = (jnp.arange(OWNERS * OBS_DEV, dtype=jnp.int32) // OBS_DEV)[None, :]
    capacity = counts[source, target]
    slot_index = jax.random.randint(jax.random.fold_in(key, 14), (4, OWNERS * OBS_DEV), 0, 1 << 20) % capacity
    result = source * SLOTS + slot_index
    result = result.at[0, receiver * OBS_DEV].set(OWNERS * SLOTS - 1)
    return result.astype(jnp.int32)


def draw_obs_count(key, part):
    counts = jax.random.randint(jax.random.fold_in(key, 15), (OWNERS,), OBS_DEV // 8, OBS_DEV + 1)
    busiest = jax.random.randint(jax.random.fold_in(key, 16), (), 0, OWNERS)
    offset = jax.random.randint(jax.random.fold_in(key, 17), (), 0, OWNERS - 1)
    lightest = (busiest + 1 + offset) % OWNERS
    counts = counts.at[lightest].set(OBS_DEV // 8)
    counts = counts.at[busiest].set(OBS_DEV)
    return counts.astype(jnp.int32)


def levels(stream_key, extent, cuts, smallest, largest):
    level = 1.0
    for axis_at, blocks in cuts:
        heights = jax.random.uniform(jax.random.fold_in(jax.random.fold_in(stream_key, 6), axis_at), (blocks,), jnp.float32, smallest / len(cuts), largest / len(cuts))
        level = level * jnp.repeat(jnp.exp(heights), extent[axis_at] // blocks).reshape((-1,) + (1,) * (len(extent) - 1 - axis_at))
    return level


def noise(own_key, dims, scale, limit, shards=(), kind=jnp.bfloat16):
    values = jax.random.normal(own_key, dims, jnp.float32) * scale
    if len(shards) > 0:
        values = levels(own_key, dims, shards, -0.22, 0.18) * values
    return jnp.clip(values, min=-limit, max=limit).astype(kind)


def setup_inputs(seed: int = 0) -> dict:
    streams_of = jax.random.split(jax.random.key(seed), 9)
    length_scale = jnp.clip(jnp.exp(math.log(1.0) - 1.0498221 * jax.random.uniform(streams_of[0], (NX, NY, LEV), jnp.float32) ** levels(streams_of[0], (NX, NY, LEV), ((0, 16), (1, 8)), -0.2, 0.2)), 0.35, 1.0)
    innovation = noise(streams_of[1], (OBS,), 1.0, 6.0, ((0, 128),), jnp.float32)
    observed_precision = jnp.clip(jnp.exp(math.log(4.0) - 2.7725887 * jax.random.uniform(streams_of[2], (OBS,), jnp.float32) ** levels(streams_of[2], (OBS,), ((0, 128),), -0.2, 0.2)), 0.25, 4.0)
    profile_weight = noise(streams_of[3], (OBS, LEV), LEV ** -0.5, 0.5, ((0, 128),), jnp.float32)
    stencil_weight = jnp.clip(0.05 + 0.39999999 * jax.random.uniform(streams_of[4], (4, OBS), jnp.float32) ** levels(streams_of[4], (4, OBS), ((1, 128),), -0.2, 0.2), 0.05, 0.45)
    send_rows = draw_send_rows(jax.random.fold_in(streams_of[8], 71), 0)
    stencil_rows = draw_stencil_rows(jax.random.fold_in(streams_of[8], 71), 0)
    obs_count = draw_obs_count(jax.random.fold_in(streams_of[8], 71), 0)
    return {"length_scale": length_scale, "innovation": innovation, "observed_precision": observed_precision, "profile_weight": profile_weight, "stencil_weight": stencil_weight, "send_rows": send_rows, "stencil_rows": stencil_rows, "obs_count": obs_count}


coupling = 0.12


def diffuse_once(padded, scales):
    centre = padded[1:-1, 1:-1]
    middle = scales[1:-1, 1:-1]
    fluxes = middle * scales[2:, 1:-1] * (centre - padded[2:, 1:-1])
    fluxes = fluxes + middle * scales[:-2, 1:-1] * (centre - padded[:-2, 1:-1])
    fluxes = fluxes + middle * scales[1:-1, 2:] * (centre - padded[1:-1, 2:])
    fluxes = fluxes + middle * scales[1:-1, :-2] * (centre - padded[1:-1, :-2])
    return centre - coupling * fluxes


def smooth(field, scales_pad):
    for sweep_index in range(PASSES):
        padded = jnp.pad(field, ((1, 1), (1, 1), (0, 0)))
        field = diffuse_once(padded, scales_pad)
    return field


def to_tiles(field):
    blocks = field.reshape(N_GX, CX, N_GY, CY, LEV).transpose(0, 2, 1, 3, 4)
    return blocks.reshape(OWNERS * CX * CY, LEV)


def from_tiles(flat):
    blocks = flat.reshape(N_GX, N_GY, CX, CY, LEV).transpose(0, 2, 1, 3, 4)
    return blocks.reshape(NX, NY, LEV)


def reference(length_scale, innovation, observed_precision, profile_weight, stencil_weight, send_rows, stencil_rows, obs_count):
    scales_pad = jnp.pad(length_scale, ((1, 1), (1, 1), (0, 0)))
    owner_numbers = jnp.arange(OWNERS, dtype=jnp.int32)
    positions = stencil_rows.reshape(4, OWNERS, OBS_DEV).astype(jnp.int32)
    source = positions // SLOTS
    slot_index = positions % SLOTS
    column = send_rows[source, owner_numbers[None, :, None], slot_index]
    global_rows = (source * (CX * CY) + column).astype(jnp.int32).transpose(1, 0, 2)
    weights = stencil_weight.reshape(4, OWNERS, OBS_DEV).transpose(1, 0, 2)
    profiles = profile_weight.reshape(OWNERS, OBS_DEV, LEV)
    live = (jnp.arange(OBS_DEV, dtype=jnp.int32)[None, :] < obs_count[:, None]).astype(jnp.float32)
    precision = live * observed_precision.reshape(OWNERS, OBS_DEV)

    def observe(field):
        flat = to_tiles(field)

        def one_owner(items):
            rows_here, weights_here, profile_here = items
            gathered = weights_here[0][:, None] * flat[rows_here[0]]
            for corner in range(1, 4):
                gathered = gathered + weights_here[corner][:, None] * flat[rows_here[corner]]
            return jnp.sum(profile_here * gathered, axis=1)

        return lax.map(one_owner, (global_rows, weights, profiles))

    def adjoint(forcing):
        def add_owner(total, items):
            rows_here, weights_here, profile_here, forcing_here = items
            spread_rows = profile_here * forcing_here[:, None]
            for corner in range(4):
                total = total.at[rows_here[corner]].add(weights_here[corner][:, None] * spread_rows)
            return total, None

        start = jnp.zeros((OWNERS * CX * CY, LEV), jnp.float32)
        total, unused = lax.scan(add_owner, start, (global_rows, weights, profiles, forcing))
        return from_tiles(total)

    right = smooth(adjoint(precision * innovation.reshape(OWNERS, OBS_DEV)), scales_pad)
    control = jnp.zeros_like(right)
    increment = jnp.zeros_like(right)
    residual = right
    direction = right
    norm_now = jnp.sum(residual * residual)
    for iteration in range(ITERS):
        smoothed = smooth(direction, scales_pad)
        image = direction + smooth(adjoint(precision * observe(smoothed)), scales_pad)
        step_length = norm_now / jnp.sum(direction * image)
        control = control + step_length * direction
        increment = increment + step_length * smoothed
        residual = residual - step_length * image
        if iteration + 1 < ITERS:
            norm_next = jnp.sum(residual * residual)
            direction = residual + (norm_next / norm_now) * direction
            norm_now = norm_next
    return control, increment
```

```python
import jax
import jax.numpy as jnp
from jax import lax
from jax.experimental import pallas as pl
from jax.experimental.pallas import tpu as pltpu
from jax.sharding import PartitionSpec as P


MIB = 1 << 20
COUPLING = 0.12
PASSES = 4
HALO = 2 * PASSES
CHUNK = 256
bf16 = jnp.bfloat16
f32 = jnp.float32


def mm(lhs, rhs):
    return jnp.dot(lhs, rhs, preferred_element_type=f32)


def halves(values):
    high = values.astype(bf16)
    return high, (values - high.astype(f32)).astype(bf16)


def live_precision(count_ref, precision_ref, step):
    place = step * CHUNK + lax.broadcasted_iota(jnp.int32, (1, CHUNK), 1)
    return jnp.where(place < count_ref[0], precision_ref[...], 0.0)


def spread_pair(profile, forcing):
    column = jnp.broadcast_to(forcing, (profile.shape[1], CHUNK)).T
    return jnp.concatenate(halves(profile * column), axis=1)


def build_kernel(
    count_ref, rows_ref, weights_ref, innovation_ref, precision_ref, profile_ref,
    high_ref, low_ref, out_ref, total_ref,
):
    step = pl.program_id(0)
    forcing = live_precision(count_ref, precision_ref, step) * innovation_ref[...]
    pair = spread_pair(profile_ref[...], forcing)
    rows = [rows_ref[k : k + 1, :] for k in range(4)]
    weights = [weights_ref[k : k + 1, :] for k in range(4)]
    for k in range(1, 4):
        for j in range(k):
            same = rows[k] == rows[j]
            weights[j] = weights[j] + jnp.where(same, weights[k], 0.0)
            weights[k] = jnp.where(same, 0.0, weights[k])

    @pl.when(step == 0)
    def _():
        total_ref[...] = jnp.zeros_like(total_ref)

    def one(index, carry):
        base = pl.multiple_of(index * CHUNK, CHUNK)
        slot = base + lax.broadcasted_iota(jnp.int32, (CHUNK, CHUNK), 0)
        matrix = jnp.zeros((CHUNK, CHUNK), f32)
        for k in (3, 2, 1, 0):
            matrix = jnp.where(rows[k] == slot, weights[k], matrix)
        high, low = halves(matrix)
        high_ref[0, pl.ds(base, CHUNK), :] = high
        low_ref[0, pl.ds(base, CHUNK), :] = low
        total_ref[pl.ds(base, CHUNK), :] += mm(high, pair) + mm(low, pair)
        return carry

    lax.fori_loop(0, total_ref.shape[0] // CHUNK, one, 0)

    @pl.when(step == pl.num_programs(0) - 1)
    def _():
        levels = out_ref.shape[1]
        out_ref[...] = total_ref[:, :levels] + total_ref[:, levels:]


def transpose_pair(received_ref, turned_ref):
    levels = received_ref.shape[1]

    def one(index, carry):
        base = pl.multiple_of(index * levels, levels)
        high, low = halves(received_ref[pl.ds(base, levels), :].T)
        turned_ref[:levels, pl.ds(base, levels)] = high
        turned_ref[levels:, pl.ds(base, levels)] = low
        return carry

    lax.fori_loop(0, received_ref.shape[0] // levels, one, 0)


def observe(turned_ref, high_ref, low_ref, profile):
    levels = profile.shape[1]
    both = mm(turned_ref[...], high_ref[0]) + mm(turned_ref[...], low_ref[0])
    return jnp.sum(profile.T * (both[:levels] + both[levels:]), axis=0, keepdims=True)


def observe_adjoint_kernel(
    count_ref, received_ref, high_ref, low_ref, precision_ref, profile_ref,
    out_ref, turned_ref, total_ref,
):
    step = pl.program_id(0)

    @pl.when(step == 0)
    def _():
        transpose_pair(received_ref, turned_ref)
        total_ref[...] = jnp.zeros_like(total_ref)

    profile = profile_ref[...]
    seen = observe(turned_ref, high_ref, low_ref, profile)
    pair = spread_pair(profile, live_precision(count_ref, precision_ref, step) * seen)

    def one(index, carry):
        base = pl.multiple_of(index * CHUNK, CHUNK)
        total_ref[pl.ds(base, CHUNK), :] += mm(
            high_ref[0, pl.ds(base, CHUNK), :], pair
        ) + mm(low_ref[0, pl.ds(base, CHUNK), :], pair)
        return carry

    lax.fori_loop(0, total_ref.shape[0] // CHUNK, one, 0)

    @pl.when(step == pl.num_programs(0) - 1)
    def _():
        levels = out_ref.shape[1]
        out_ref[...] = total_ref[:, :levels] + total_ref[:, levels:]


def observe_norm_kernel(
    count_ref, received_ref, high_ref, low_ref, precision_ref, profile_ref, first_ref, second_ref,
    out_ref, turned_ref, total_ref,
):
    step = pl.program_id(0)

    @pl.when(step == 0)
    def _():
        transpose_pair(received_ref, turned_ref)
        total_ref[...] = jnp.zeros_like(total_ref)

    seen = observe(turned_ref, high_ref, low_ref, profile_ref[...])
    total_ref[...] += live_precision(count_ref, precision_ref, step) * seen * seen

    @pl.when(step == pl.num_programs(0) - 1)
    def _():
        lane = lax.broadcasted_iota(jnp.int32, out_ref.shape, 1)
        parts = (first_ref[0], second_ref[0], second_ref[1], total_ref[...])
        row = jnp.zeros(out_ref.shape, f32)
        for k in range(4):
            row = jnp.where(lane == k, jnp.sum(parts[k]), row)
        out_ref[...] = row


def place_kernel(send_ref, arrived_ref, out_ref, pair_ref):
    slots, levels = arrived_ref.shape

    def split(index, carry):
        base = pl.multiple_of(index * CHUNK, CHUNK)
        high, low = halves(arrived_ref[pl.ds(base, CHUNK), :])
        pair_ref[pl.ds(base, CHUNK), :levels] = high
        pair_ref[pl.ds(base, CHUNK), levels:] = low
        return carry

    lax.fori_loop(0, slots // CHUNK, split, 0)
    size = 128

    def one(index, carry):
        base = pl.multiple_of(index * size, size)
        column = base + lax.broadcasted_iota(jnp.int32, (size, slots), 0)
        matrix = jnp.where(column == send_ref[...], 1.0, 0.0).astype(bf16)
        both = mm(matrix, pair_ref[...])
        out_ref[pl.ds(base, size), :] = both[:, :levels] + both[:, levels:]
        return carry

    lax.fori_loop(0, out_ref.shape[0] // size, one, 0)


def smooth_kernel(
    send_ref, centre_ref, up_ref, down_ref, left_ref, right_ref,
    scale_ref, scale_up_ref, scale_down_ref, scale_left_ref, scale_right_ref,
    *rest,
):
    *given, half_ref, full_ref, out_ref, sums_ref, field, east, north = rest
    across, along, levels = centre_ref.shape
    wide, tall = across + 2 * HALO, along + 2 * HALO

    def fill(target, middle, above, below, west, easterly):
        target[HALO : HALO + across, HALO : HALO + along] = middle[...]
        target[:HALO, HALO : HALO + along] = above[...]
        target[HALO + across :, HALO : HALO + along] = below[...]
        target[:, :HALO] = west[...]
        target[:, HALO + along :] = easterly[...]

    fill(field, scale_ref, scale_up_ref, scale_down_ref, scale_left_ref, scale_right_ref)

    def conductance(i, carry):
        here = COUPLING * field[i]
        after = field[jnp.minimum(i + 1, wide - 1)]
        east[i] = here * after
        north[i, : tall - 1] = here[: tall - 1] * field[i, 1:]
        north[i, tall - 1 :] = jnp.zeros((1, levels), f32)
        return carry

    lax.fori_loop(0, wide, conductance, 0)
    fill(field, centre_ref, up_ref, down_ref, left_ref, right_ref)

    def sweep(k):
        def row(i, carry):
            here, inward = carry
            after = field[i + 1, 1:-1]
            outward = east[i, 1:-1] * (after - here)
            above = north[i, 1:-1] * (field[i, 2:] - here)
            below = north[i, :-2] * (here - field[i, :-2])
            field[i, 1:-1] = here + ((outward - inward) + (above - below))
            return after, outward

        here = field[k, 1:-1]
        lax.fori_loop(k, wide - k, row, (here, east[k - 1, 1:-1] * (here - field[k - 1, 1:-1])))

    def middle():
        return field[HALO : HALO + across, HALO : HALO + along]

    for k in range(1, PASSES + 1):
        sweep(k)
    half = middle()
    half_ref[...] = half
    if given:
        sums_ref[0] = jnp.sum((given[0][...] * half).reshape(-1, 8, levels), axis=0)
        sums_ref[1] = jnp.sum((half * half).reshape(-1, 8, levels), axis=0)
    else:
        sums_ref[0] = jnp.sum((half * half).reshape(-1, 8, levels), axis=0)
    for k in range(PASSES + 1, HALO + 1):
        sweep(k)
    full = middle()
    full_ref[...] = full
    columns = across * along
    pair = jnp.concatenate(halves(full.reshape(columns, levels)), axis=1)

    def gather(index, carry):
        base = pl.multiple_of(index * levels, levels)
        wanted = jnp.broadcast_to(send_ref[:, pl.ds(base, levels)].astype(f32), (levels, levels)).T
        lane = lax.broadcasted_iota(jnp.int32, (levels, levels), 1).astype(f32)
        matrix = jnp.concatenate(
            [jnp.where(wanted == lane + q, 1.0, 0.0).astype(bf16) for q in range(0, columns, levels)],
            axis=1,
        )
        both = mm(matrix, pair)
        out_ref[pl.ds(base, levels), :] = both[:, :levels] + both[:, levels:]
        return carry

    lax.fori_loop(0, out_ref.shape[0] // levels, gather, 0)


def finish_kernel(sums_ref, b_ref, sb_ref, p_ref, sp_ref, control_ref, increment_ref):
    total = jnp.sum(sums_ref[...], axis=0, keepdims=True)
    lane = lax.broadcasted_iota(jnp.int32, total.shape, 1)
    a, c, e, f = [jnp.sum(jnp.where(lane == k, total, 0.0), axis=1, keepdims=True) for k in range(4)]
    slope = c / a
    first = 1.0 / (1.0 + slope)
    rest = e / a - slope * slope
    ratio = first * first * rest
    curved = rest + (f / a - 2.0 * slope * (e / a) + slope * slope * slope)
    second = ratio / (first * first * curved - ratio * ratio * (1.0 + slope))
    of_b = first + second * (ratio + first * slope)
    of_p = -second * first
    control_ref[...] = of_b * b_ref[...] + of_p * p_ref[...]
    increment_ref[...] = of_b * sb_ref[...] + of_p * sp_ref[...]


def step_from(cells, axis, up):
    count = lax.axis_size(axis)
    pairs = [(i, i + 1) if up else (i + 1, i) for i in range(count - 1)]
    return lax.ppermute(cells, axis, pairs)


def rims(cells):
    along = cells.shape[1]
    up = step_from(cells, "gx", True)
    down = step_from(cells, "gx", False)
    tail = jnp.concatenate([x[:, along - HALO :] for x in (up, cells, down)], axis=0)
    head = jnp.concatenate([x[:, :HALO] for x in (up, cells, down)], axis=0)
    return up, down, step_from(tail, "gy", True), step_from(head, "gy", False)


def exchange(rows):
    return lax.all_to_all(rows, ("gx", "gy"), split_axis=0, concat_axis=0, tiled=True)


def params(mib):
    return pltpu.CompilerParams(vmem_limit_bytes=mib * MIB)


def on_device(
    length_scale, innovation, observed_precision, profile_weight, stencil_weight, send_rows, stencil_rows, obs_count,
):
    across, along, levels = length_scale.shape
    owners, slot_count = send_rows.shape[1:]
    slots = owners * slot_count
    columns = across * along
    obs = innovation.shape[0]
    steps = obs // CHUNK
    send = send_rows.reshape(1, slots)
    innovation = innovation.reshape(1, obs)
    precision = observed_precision.reshape(1, obs)
    scale_rims = rims(length_scale)

    whole = pl.BlockSpec(memory_space=pltpu.VMEM)
    scalar = pl.BlockSpec(memory_space=pltpu.SMEM)
    four = pl.BlockSpec((4, CHUNK), lambda i: (0, i))
    line = pl.BlockSpec((1, CHUNK), lambda i: (0, i))
    profile = pl.BlockSpec((CHUNK, levels), lambda i: (i, 0))
    block = pl.BlockSpec((1, slots, CHUNK), lambda i: (i, 0, 0))
    rows_all = pl.BlockSpec((slots, levels), lambda i: (0, 0))
    half_matrix = jax.ShapeDtypeStruct((steps, slots, CHUNK), bf16)
    slot_rows = jax.ShapeDtypeStruct((slots, levels), f32)
    tile = jax.ShapeDtypeStruct((across, along, levels), f32)

    def trade(rows):
        return exchange(rows.reshape(owners, slot_count, levels)).reshape(slots, levels)

    def to_columns(arrived):
        return pl.pallas_call(
            place_kernel,
            out_shape=jax.ShapeDtypeStruct((columns, levels), f32),
            in_specs=[whole, whole],
            out_specs=whole,
            scratch_shapes=[pltpu.VMEM((slots, 2 * levels), bf16)],
            compiler_params=params(24),
            name="place",
        )(send, arrived).reshape(across, along, levels)

    def smooth_twice(cells, given):
        grown = (across + 2 * HALO, along + 2 * HALO, levels)
        count = 1 + len(given)
        return pl.pallas_call(
            smooth_kernel,
            out_shape=(tile, tile, slot_rows, jax.ShapeDtypeStruct((count, 8, levels), f32)),
            in_specs=[whole] * (11 + len(given)),
            out_specs=(whole,) * 4,
            scratch_shapes=[pltpu.VMEM(grown, f32)] * 3,
            compiler_params=params(24),
            name="smooth",
        )(send, cells, *rims(cells), length_scale, *scale_rims, *given)

    high, low, spread = pl.pallas_call(
        build_kernel,
        grid=(steps,),
        out_shape=(half_matrix, half_matrix, slot_rows),
        in_specs=[scalar, four, four, line, line, profile],
        out_specs=(block, block, rows_all),
        scratch_shapes=[pltpu.VMEM((slots, 2 * levels), f32)],
        compiler_params=params(32),
        name="build",
    )(obs_count, stencil_rows, stencil_weight, innovation, precision, profile_weight)

    b, sb, outgoing, first_sums = smooth_twice(to_columns(trade(spread)), ())

    spread = pl.pallas_call(
        observe_adjoint_kernel,
        grid=(steps,),
        out_shape=slot_rows,
        in_specs=[scalar, rows_all, block, block, line, profile],
        out_specs=rows_all,
        scratch_shapes=[pltpu.VMEM((2 * levels, slots), bf16), pltpu.VMEM((slots, 2 * levels), f32)],
        compiler_params=params(32),
        name="observe_adjoint",
    )(obs_count, trade(outgoing), high, low, precision, profile_weight)

    p, sp, outgoing, second_sums = smooth_twice(to_columns(trade(spread)), (b,))

    sums = pl.pallas_call(
        observe_norm_kernel,
        grid=(steps,),
        out_shape=jax.ShapeDtypeStruct((owners, levels), f32),
        in_specs=[
            scalar, rows_all, block, block, line, profile,
            pl.BlockSpec((1, 8, levels), lambda i: (0, 0, 0)),
            pl.BlockSpec((2, 8, levels), lambda i: (0, 0, 0)),
        ],
        out_specs=pl.BlockSpec((owners, levels), lambda i: (0, 0)),
        scratch_shapes=[pltpu.VMEM((2 * levels, slots), bf16), pltpu.VMEM((1, CHUNK), f32)],
        compiler_params=params(32),
        name="observe_norm",
    )(obs_count, trade(outgoing), high, low, precision, profile_weight, first_sums, second_sums)

    sums = exchange(sums.reshape(owners, 1, levels)).reshape(owners, levels)

    return pl.pallas_call(
        finish_kernel,
        out_shape=(
            jax.ShapeDtypeStruct((columns, levels), f32),
            jax.ShapeDtypeStruct((columns, levels), f32),
        ),
        in_specs=[whole] * 5,
        out_specs=(whole, whole),
        compiler_params=params(16),
        name="finish",
    )(sums, *(x.reshape(columns, levels) for x in (b, sb, p, sp)))


def solution(mesh):
    def run(*args):
        control, increment = on_device(*args)
        shape = args[0].shape
        return control.reshape(shape), increment.reshape(shape)

    return jax.shard_map(
        run,
        mesh=mesh,
        in_specs=(
            P("gx", "gy", None),
            P(("gx", "gy")),
            P(("gx", "gy")),
            P(("gx", "gy"), None),
            P(None, ("gx", "gy")),
            P(("gx", "gy"), None, None),
            P(None, ("gx", "gy")),
            P(("gx", "gy")),
        ),
        out_specs=(P("gx", "gy", None), P("gx", "gy", None)),
        check_vma=False,
    )
```

```python
import jax
import jax.numpy as jnp
from jax import lax
from jax.experimental import pallas as pl
from jax.experimental.pallas import tpu as pltpu
from jax.sharding import PartitionSpec as P


MIB = 1 << 20
COUPLING = 0.12
PASSES = 4
HALO = 2 * PASSES
CHUNK = 256
bf16 = jnp.bfloat16
f32 = jnp.float32


def mm(lhs, rhs):
    return jnp.dot(lhs, rhs, preferred_element_type=f32)


def halves(values):
    high = values.astype(bf16)
    return high, (values - high.astype(f32)).astype(bf16)


def live_precision(count_ref, precision_ref):
    place = lax.broadcasted_iota(jnp.int32, precision_ref.shape, 1)
    return jnp.where(place < count_ref[0], precision_ref[...], 0.0)


def matrix_kernel(rows_hbm, weights_hbm, out_ref, rows_ref, weights_ref, sems):
    copies = [
        pltpu.make_async_copy(rows_hbm, rows_ref, sems.at[0]),
        pltpu.make_async_copy(weights_hbm, weights_ref, sems.at[1]),
    ]
    for copy in copies:
        copy.start()
    for copy in copies:
        copy.wait()
    slots, obs = out_ref.shape[0], rows_ref.shape[1]
    rows = [rows_ref[k : k + 1, :] for k in range(4)]
    weights = [weights_ref[k : k + 1, :] for k in range(4)]
    for k in range(1, 4):
        for j in range(k):
            same = rows[k] == rows[j]
            weights[j] = weights[j] + jnp.where(same, weights[k], 0.0)
            weights[k] = jnp.where(same, 0.0, weights[k])
    parts = [halves(weight) for weight in weights]
    shape = (CHUNK, CHUNK)
    slot = lax.broadcasted_iota(jnp.int32, shape, 0).astype(f32).astype(bf16)

    def one(index, carry):
        base = pl.multiple_of(index * CHUNK, CHUNK)
        near = [(row - base).astype(f32).astype(bf16) for row in rows]
        for at in range(0, obs, CHUNK):
            high = jnp.zeros(shape, bf16)
            low = jnp.zeros(shape, bf16)
            for k in (3, 2, 1, 0):
                cut = slice(at, at + CHUNK)
                hit = jnp.broadcast_to(near[k][:, cut], shape) == slot
                high = jnp.where(hit, jnp.broadcast_to(parts[k][0][:, cut], shape), high)
                low = jnp.where(hit, jnp.broadcast_to(parts[k][1][:, cut], shape), low)
            out_ref[pl.ds(base, CHUNK), at : at + CHUNK] = high
            out_ref[pl.ds(base, CHUNK), obs + at : obs + at + CHUNK] = low
        return carry

    lax.fori_loop(0, slots // CHUNK, one, 0)


def spread_rows(matrix_ref, pair_ref, out_ref):
    levels = out_ref.shape[1]
    size = 4 * CHUNK

    def one(index, carry):
        base = pl.multiple_of(index * size, size)
        both = mm(matrix_ref[pl.ds(base, size), :], pair_ref[...])
        out_ref[pl.ds(base, size), :] = both[:, :levels] + both[:, levels:]
        return carry

    lax.fori_loop(0, out_ref.shape[0] // size, one, 0)


def fill_pair(profile_ref, forcing, pair_ref):
    obs, levels = profile_ref.shape
    for at in range(0, obs, levels):
        column = jnp.broadcast_to(forcing[:, at : at + levels], (levels, levels)).T
        high, low = halves(profile_ref[at : at + levels, :] * column)
        for base in (at, obs + at):
            pair_ref[base : base + levels, :levels] = high
            pair_ref[base : base + levels, levels:] = low


def spread_kernel(count_ref, innovation_ref, precision_ref, profile_ref, matrix_ref, out_ref, pair_ref):
    forcing = live_precision(count_ref, precision_ref) * innovation_ref[...]
    fill_pair(profile_ref, forcing, pair_ref)
    spread_rows(matrix_ref, pair_ref, out_ref)


def observe(received_ref, matrix_ref, profile_ref, turned_ref, seen_ref):
    slots, levels = received_ref.shape
    obs = profile_ref.shape[0]
    for at in range(0, slots, levels):
        high, low = halves(received_ref[at : at + levels, :].T)
        turned_ref[:levels, at : at + levels] = high
        turned_ref[levels:, at : at + levels] = low
    size = 4 * CHUNK

    def one(index, carry):
        base = pl.multiple_of(index * size, size)
        both = mm(turned_ref[...], matrix_ref[:, pl.ds(base, size)])
        gathered = both[:levels] + both[levels:]
        gathered = gathered + mm(
            turned_ref[:levels], matrix_ref[:, pl.ds(pl.multiple_of(obs + index * size, size), size)]
        )
        seen_ref[:, pl.ds(base, size)] = jnp.sum(
            profile_ref[pl.ds(base, size), :].T * gathered, axis=0, keepdims=True
        )
        return carry

    lax.fori_loop(0, obs // size, one, 0)


def observe_adjoint_kernel(
    count_ref, received_ref, precision_ref, profile_ref, matrix_ref, out_ref, turned_ref, seen_ref, pair_ref,
):
    observe(received_ref, matrix_ref, profile_ref, turned_ref, seen_ref)
    fill_pair(profile_ref, live_precision(count_ref, precision_ref) * seen_ref[...], pair_ref)
    spread_rows(matrix_ref, pair_ref, out_ref)


def observe_norm_kernel(
    count_ref, received_ref, precision_ref, profile_ref, matrix_ref, first_ref, second_ref,
    out_ref, turned_ref, seen_ref,
):
    observe(received_ref, matrix_ref, profile_ref, turned_ref, seen_ref)
    seen = seen_ref[...]
    lane = lax.broadcasted_iota(jnp.int32, out_ref.shape, 1)
    parts = (first_ref[0], second_ref[0], second_ref[1], live_precision(count_ref, precision_ref) * seen * seen)
    row = jnp.zeros(out_ref.shape, f32)
    for k in range(4):
        row = jnp.where(lane == k, jnp.sum(parts[k]), row)
    out_ref[...] = row


def place_kernel(send_ref, arrived_ref, out_ref, pair_ref):
    slots, levels = arrived_ref.shape

    def split(index, carry):
        base = pl.multiple_of(index * CHUNK, CHUNK)
        high, low = halves(arrived_ref[pl.ds(base, CHUNK), :])
        pair_ref[pl.ds(base, CHUNK), :levels] = high
        pair_ref[pl.ds(base, CHUNK), levels:] = low
        return carry

    lax.fori_loop(0, slots // CHUNK, split, 0)
    size = 128

    def one(index, carry):
        base = pl.multiple_of(index * size, size)
        column = base + lax.broadcasted_iota(jnp.int32, (size, slots), 0)
        matrix = jnp.where(column == send_ref[...], 1.0, 0.0).astype(bf16)
        both = mm(matrix, pair_ref[...])
        out_ref[pl.ds(base, size), :] = both[:, :levels] + both[:, levels:]
        return carry

    lax.fori_loop(0, out_ref.shape[0] // size, one, 0)


def strip_kernel(place_ref, cells_ref, one_ref, two_ref, first_ref, second_ref):
    across, along, _ = cells_ref.shape
    odd = place_ref[1]
    head_or_tail = pl.multiple_of((1 - odd) * (along - HALO), HALO)
    tail_or_head = pl.multiple_of(odd * (along - HALO), HALO)
    for target, at in ((first_ref, head_or_tail), (second_ref, tail_or_head)):
        for k, source in enumerate((one_ref, cells_ref, two_ref)):
            target[k * across : (k + 1) * across] = source[:, pl.ds(at, HALO), :]


def fill(place_ref, target, cells_ref, one_ref, two_ref, first_ref, second_ref):
    across, along, _ = cells_ref.shape
    odd_x, odd_y = place_ref[0], place_ref[1]
    above = (1 - odd_x) * (across + HALO)
    below = odd_x * (across + HALO)
    target[HALO : HALO + across, HALO : HALO + along] = cells_ref[...]
    target[pl.ds(above, HALO), HALO : HALO + along] = one_ref[...]
    target[pl.ds(below, HALO), HALO : HALO + along] = two_ref[...]
    for source, at in ((first_ref, 1 - odd_y), (second_ref, odd_y)):
        start = pl.multiple_of(at * (along + HALO), HALO)
        for k, row in enumerate((above, HALO, below)):
            target[pl.ds(row, HALO), pl.ds(start, HALO), :] = source[k * across : (k + 1) * across]


def conduct_kernel(place_ref, cells_ref, one_ref, two_ref, first_ref, second_ref, east_ref, north_ref, field):
    wide, tall, levels = field.shape
    across, along, _ = cells_ref.shape
    fill(place_ref, field, cells_ref, one_ref, two_ref, first_ref, second_ref)
    edges = (place_ref[2] == 0, place_ref[2] == place_ref[4] - 1, place_ref[3] == 0, place_ref[3] == place_ref[5] - 1)

    @pl.when(edges[0])
    def _():
        field[:HALO] = jnp.zeros((HALO, tall, levels), f32)

    @pl.when(edges[1])
    def _():
        field[HALO + across :] = jnp.zeros((HALO, tall, levels), f32)

    @pl.when(edges[2])
    def _():
        field[:, :HALO] = jnp.zeros((wide, HALO, levels), f32)

    @pl.when(edges[3])
    def _():
        field[:, HALO + along :] = jnp.zeros((wide, HALO, levels), f32)

    def one(i, carry):
        here = COUPLING * field[i]
        after = field[jnp.minimum(i + 1, wide - 1)]
        east_ref[i] = here * after
        north_ref[i, : tall - 1] = here[: tall - 1] * field[i, 1:]
        north_ref[i, tall - 1 :] = jnp.zeros((1, levels), f32)
        return carry

    lax.fori_loop(0, wide, one, 0)


def smooth_kernel(place_ref, send_ref, cells_ref, one_ref, two_ref, first_ref, second_ref, east, north, *rest):
    *given, half_ref, full_ref, out_ref, sums_ref, field = rest
    across, along, levels = cells_ref.shape
    wide = across + 2 * HALO
    fill(place_ref, field, cells_ref, one_ref, two_ref, first_ref, second_ref)

    def sweep(k):
        def row(i, carry):
            here, inward = carry
            after = field[i + 1, 1:-1]
            outward = east[i, 1:-1] * (after - here)
            above = north[i, 1:-1] * (field[i, 2:] - here)
            below = north[i, :-2] * (here - field[i, :-2])
            field[i, 1:-1] = here + ((outward - inward) + (above - below))
            return after, outward

        here = field[k, 1:-1]
        lax.fori_loop(k, wide - k, row, (here, east[k - 1, 1:-1] * (here - field[k - 1, 1:-1])))

    def middle():
        return field[HALO : HALO + across, HALO : HALO + along]

    for k in range(1, PASSES + 1):
        sweep(k)
    half = middle()
    half_ref[...] = half
    if given:
        sums_ref[0] = jnp.sum((given[0][...] * half).reshape(-1, 8, levels), axis=0)
        sums_ref[1] = jnp.sum((half * half).reshape(-1, 8, levels), axis=0)
    else:
        sums_ref[0] = jnp.sum((half * half).reshape(-1, 8, levels), axis=0)
    for k in range(PASSES + 1, HALO + 1):
        sweep(k)
    full = middle()
    full_ref[...] = full
    columns = across * along
    pair = jnp.concatenate(halves(full.reshape(columns, levels)), axis=1)

    def gather(index, carry):
        base = pl.multiple_of(index * levels, levels)
        wanted = jnp.broadcast_to(send_ref[:, pl.ds(base, levels)].astype(f32), (levels, levels)).T
        lane = lax.broadcasted_iota(jnp.int32, (levels, levels), 1).astype(f32)
        matrix = jnp.concatenate(
            [jnp.where(wanted == lane + q, 1.0, 0.0).astype(bf16) for q in range(0, columns, levels)],
            axis=1,
        )
        both = mm(matrix, pair)
        out_ref[pl.ds(base, levels), :] = both[:, :levels] + both[:, levels:]
        return carry

    lax.fori_loop(0, out_ref.shape[0] // levels, gather, 0)


def finish_kernel(sums_ref, b_ref, sb_ref, p_ref, sp_ref, control_ref, increment_ref):
    total = jnp.sum(sums_ref[...], axis=0, keepdims=True)
    lane = lax.broadcasted_iota(jnp.int32, total.shape, 1)
    a, c, e, f = [jnp.sum(jnp.where(lane == k, total, 0.0), axis=1, keepdims=True) for k in range(4)]
    slope = c / a
    first = 1.0 / (1.0 + slope)
    rest = e / a - slope * slope
    ratio = first * first * rest
    curved = rest + (f / a - 2.0 * slope * (e / a) + slope * slope * slope)
    second = ratio / (first * first * curved - ratio * ratio * (1.0 + slope))
    of_b = first + second * (ratio + first * slope)
    of_p = -second * first
    control_ref[...] = of_b * b_ref[...] + of_p * p_ref[...]
    increment_ref[...] = of_b * sb_ref[...] + of_p * sp_ref[...]


def swap(cells, axis, odd):
    count = lax.axis_size(axis)
    pairs = [(i, (i + 1) % count) for i in range(odd, count, 2)]
    return lax.ppermute(cells, axis, pairs + [(j, i) for i, j in pairs])


def exchange(rows):
    return lax.all_to_all(rows, ("gx", "gy"), split_axis=0, concat_axis=0, tiled=True)


def params(mib):
    return pltpu.CompilerParams(vmem_limit_bytes=mib * MIB)


def cost(flops, size):
    return pl.CostEstimate(flops=flops, bytes_accessed=size, transcendentals=0)


def on_device(
    length_scale, innovation, observed_precision, profile_weight, stencil_weight, send_rows, stencil_rows, obs_count,
):
    across, along, levels = length_scale.shape
    owners, slot_count = send_rows.shape[1:]
    slots = owners * slot_count
    columns = across * along
    obs = innovation.shape[0]
    send = send_rows.reshape(1, slots)
    innovation = innovation.reshape(1, obs)
    precision = observed_precision.reshape(1, obs)
    at_x, at_y = lax.axis_index("gx"), lax.axis_index("gy")
    sizes = [jnp.int32(lax.axis_size(axis)) for axis in ("gx", "gy")]
    place = jnp.stack([at_x % 2, at_y % 2, at_x, at_y, *sizes]).astype(jnp.int32)

    whole = pl.BlockSpec(memory_space=pltpu.VMEM)
    scalar = pl.BlockSpec(memory_space=pltpu.SMEM)
    afar = pl.BlockSpec(memory_space=pltpu.HBM)
    slot_rows = jax.ShapeDtypeStruct((slots, levels), f32)
    tile = jax.ShapeDtypeStruct((across, along, levels), f32)
    strip = jax.ShapeDtypeStruct((across + 2 * HALO, HALO, levels), f32)
    grown = (across + 2 * HALO, along + 2 * HALO, levels)
    pair_scratch = pltpu.VMEM((2 * obs, 2 * levels), bf16)
    turned_scratch = pltpu.VMEM((2 * levels, slots), bf16)
    seen_scratch = pltpu.VMEM((1, obs), f32)

    def trade(rows):
        return exchange(rows.reshape(owners, slot_count, levels)).reshape(slots, levels)

    def strips(cells, one, two):
        return pl.pallas_call(
            strip_kernel,
            out_shape=(strip, strip),
            in_specs=[scalar] + [whole] * 3,
            out_specs=(whole, whole),
            compiler_params=params(2),
            name="strips",
        )(place, cells, one, two)

    def over_x(cells):
        return swap(cells, "gx", 0), swap(cells, "gx", 1)

    def over_y(first, second):
        return swap(first, "gy", 0), swap(second, "gy", 1)

    scale_x = over_x(length_scale)
    matrix = pl.pallas_call(
        matrix_kernel,
        out_shape=jax.ShapeDtypeStruct((slots, 2 * obs), bf16),
        in_specs=[afar, afar],
        out_specs=whole,
        scratch_shapes=[
            pltpu.VMEM((4, obs), jnp.int32),
            pltpu.VMEM((4, obs), f32),
            pltpu.SemaphoreType.DMA((2,)),
        ],
        compiler_params=params(4),
        cost_estimate=cost(1 << 30, 1 << 24),
        name="matrix",
    )(*(pltpu.with_memory_space_constraint(x, pltpu.HBM) for x in (stencil_rows, stencil_weight)))
    innovation, *scale_x = lax.optimization_barrier((innovation, *scale_x))
    scale_y = over_y(*strips(length_scale, *scale_x))
    spread = pl.pallas_call(
        spread_kernel,
        out_shape=slot_rows,
        in_specs=[scalar] + [whole] * 4,
        out_specs=whole,
        scratch_shapes=[pair_scratch],
        compiler_params=params(14),
        cost_estimate=cost(8 << 30, 1 << 24),
        name="spread",
    )(obs_count, innovation, precision, profile_weight, matrix)
    spread, *scale_y = lax.optimization_barrier((spread, *scale_y))
    conductances = pl.pallas_call(
        conduct_kernel,
        out_shape=(jax.ShapeDtypeStruct(grown, f32),) * 2,
        in_specs=[scalar] + [whole] * 5,
        out_specs=(whole, whole),
        scratch_shapes=[pltpu.VMEM(grown, f32)],
        compiler_params=params(4),
        name="conduct",
    )(place, length_scale, *scale_x, *scale_y)
    spread, send, *conductances = lax.optimization_barrier((spread, send, *conductances))

    def to_columns(arrived):
        return pl.pallas_call(
            place_kernel,
            out_shape=jax.ShapeDtypeStruct((columns, levels), f32),
            in_specs=[whole, whole],
            out_specs=whole,
            scratch_shapes=[pltpu.VMEM((slots, 2 * levels), bf16)],
            compiler_params=params(8),
            name="place",
        )(send, arrived).reshape(across, along, levels)

    def smooth_twice(cells, given):
        aside = over_x(cells)
        count = 1 + len(given)
        return pl.pallas_call(
            smooth_kernel,
            out_shape=(tile, tile, slot_rows, jax.ShapeDtypeStruct((count, 8, levels), f32)),
            in_specs=[scalar] + [whole] * (8 + len(given)),
            out_specs=(whole,) * 4,
            scratch_shapes=[pltpu.VMEM(grown, f32)],
            compiler_params=params(8),
            name="smooth",
        )(place, send, cells, *aside, *over_y(*strips(cells, *aside)), *conductances, *given)

    b, sb, outgoing, first_sums = smooth_twice(to_columns(trade(spread)), ())

    spread = pl.pallas_call(
        observe_adjoint_kernel,
        out_shape=slot_rows,
        in_specs=[scalar] + [whole] * 4,
        out_specs=whole,
        scratch_shapes=[turned_scratch, seen_scratch, pair_scratch],
        compiler_params=params(16),
        name="observe_adjoint",
    )(obs_count, trade(outgoing), precision, profile_weight, matrix)

    p, sp, outgoing, second_sums = smooth_twice(to_columns(trade(spread)), (b,))

    sums = pl.pallas_call(
        observe_norm_kernel,
        out_shape=jax.ShapeDtypeStruct((owners, levels), f32),
        in_specs=[scalar] + [whole] * 6,
        out_specs=whole,
        scratch_shapes=[turned_scratch, seen_scratch],
        compiler_params=params(14),
        name="observe_norm",
    )(obs_count, trade(outgoing), precision, profile_weight, matrix, first_sums, second_sums)

    sums = exchange(sums.reshape(owners, 1, levels)).reshape(owners, levels)

    return pl.pallas_call(
        finish_kernel,
        out_shape=(
            jax.ShapeDtypeStruct((columns, levels), f32),
            jax.ShapeDtypeStruct((columns, levels), f32),
        ),
        in_specs=[whole] * 5,
        out_specs=(whole, whole),
        compiler_params=params(4),
        name="finish",
    )(sums, *(x.reshape(columns, levels) for x in (b, sb, p, sp)))


def solution(mesh):
    def run(*args):
        control, increment = on_device(*args)
        shape = args[0].shape
        return control.reshape(shape), increment.reshape(shape)

    return jax.shard_map(
        run,
        mesh=mesh,
        in_specs=(
            P("gx", "gy", None),
            P(("gx", "gy")),
            P(("gx", "gy")),
            P(("gx", "gy"), None),
            P(None, ("gx", "gy")),
            P(("gx", "gy"), None, None),
            P(None, ("gx", "gy")),
            P(("gx", "gy")),
        ),
        out_specs=(P("gx", "gy", None), P("gx", "gy", None)),
        check_vma=False,
    )
```

```python
import jax
import jax.numpy as jnp
from jax import lax
from jax.experimental import pallas as pl
from jax.experimental.pallas import tpu as pltpu
from jax.sharding import PartitionSpec as P


MIB = 1 << 20
COUPLING = 0.12
PASSES = 4
HALO = 2 * PASSES
CHUNK = 256
bf16 = jnp.bfloat16
f32 = jnp.float32


def mm(lhs, rhs):
    return jnp.dot(lhs, rhs, preferred_element_type=f32)


def halves(values):
    high = values.astype(bf16)
    return high, (values - high.astype(f32)).astype(bf16)


def live_precision(count_ref, precision_ref):
    place = lax.broadcasted_iota(jnp.int32, precision_ref.shape, 1)
    return jnp.where(place < count_ref[0], precision_ref[...], 0.0)


def matrix_kernel(rows_hbm, weights_hbm, out_ref, rows_ref, weights_ref, sems):
    copies = [
        pltpu.make_async_copy(rows_hbm, rows_ref, sems.at[0]),
        pltpu.make_async_copy(weights_hbm, weights_ref, sems.at[1]),
    ]
    for copy in copies:
        copy.start()
    for copy in copies:
        copy.wait()
    slots, obs = out_ref.shape[0], rows_ref.shape[1]
    rows = [rows_ref[k : k + 1, :] for k in range(4)]
    weights = [weights_ref[k : k + 1, :] for k in range(4)]
    for k in range(1, 4):
        for j in range(k):
            same = rows[k] == rows[j]
            weights[j] = weights[j] + jnp.where(same, weights[k], 0.0)
            weights[k] = jnp.where(same, 0.0, weights[k])
    parts = [halves(weight) for weight in weights]
    shape = (CHUNK, CHUNK)
    slot = lax.broadcasted_iota(jnp.int32, shape, 0).astype(f32).astype(bf16)

    def one(index, carry):
        base = pl.multiple_of(index * CHUNK, CHUNK)
        near = [(row - base).astype(f32).astype(bf16) for row in rows]
        for at in range(0, obs, CHUNK):
            high = jnp.zeros(shape, bf16)
            low = jnp.zeros(shape, bf16)
            for k in (3, 2, 1, 0):
                cut = slice(at, at + CHUNK)
                hit = jnp.broadcast_to(near[k][:, cut], shape) == slot
                high = jnp.where(hit, jnp.broadcast_to(parts[k][0][:, cut], shape), high)
                low = jnp.where(hit, jnp.broadcast_to(parts[k][1][:, cut], shape), low)
            out_ref[pl.ds(base, CHUNK), at : at + CHUNK] = high
            out_ref[pl.ds(base, CHUNK), obs + at : obs + at + CHUNK] = low
        return carry

    lax.fori_loop(0, slots // CHUNK, one, 0)


def spread_rows(matrix_ref, pair_ref, out_ref):
    levels = out_ref.shape[1]
    size = 4 * CHUNK

    def one(index, carry):
        base = pl.multiple_of(index * size, size)
        both = mm(matrix_ref[pl.ds(base, size), :], pair_ref[...])
        out_ref[pl.ds(base, size), :] = both[:, :levels] + both[:, levels:]
        return carry

    lax.fori_loop(0, out_ref.shape[0] // size, one, 0)


def fill_pair(profile_ref, forcing, pair_ref):
    obs, levels = profile_ref.shape
    for at in range(0, obs, levels):
        column = jnp.broadcast_to(forcing[:, at : at + levels], (levels, levels)).T
        high, low = halves(profile_ref[at : at + levels, :] * column)
        for base in (at, obs + at):
            pair_ref[base : base + levels, :levels] = high
            pair_ref[base : base + levels, levels:] = low


def spread_kernel(count_ref, innovation_ref, precision_ref, profile_ref, matrix_ref, out_ref, pair_ref):
    forcing = live_precision(count_ref, precision_ref) * innovation_ref[...]
    fill_pair(profile_ref, forcing, pair_ref)
    spread_rows(matrix_ref, pair_ref, out_ref)


def observe(received_ref, matrix_ref, profile_ref, turned_ref, seen_ref):
    slots, levels = received_ref.shape
    obs = profile_ref.shape[0]
    for at in range(0, slots, levels):
        high, low = halves(received_ref[at : at + levels, :].T)
        turned_ref[:levels, at : at + levels] = high
        turned_ref[levels:, at : at + levels] = low
    size = 4 * CHUNK

    def one(index, carry):
        base = pl.multiple_of(index * size, size)
        both = mm(turned_ref[...], matrix_ref[:, pl.ds(base, size)])
        gathered = both[:levels] + both[levels:]
        gathered = gathered + mm(
            turned_ref[:levels], matrix_ref[:, pl.ds(pl.multiple_of(obs + index * size, size), size)]
        )
        seen_ref[:, pl.ds(base, size)] = jnp.sum(
            profile_ref[pl.ds(base, size), :].T * gathered, axis=0, keepdims=True
        )
        return carry

    lax.fori_loop(0, obs // size, one, 0)


def observe_adjoint_kernel(
    count_ref, received_ref, precision_ref, profile_ref, matrix_ref, out_ref, turned_ref, seen_ref, pair_ref,
):
    observe(received_ref, matrix_ref, profile_ref, turned_ref, seen_ref)
    fill_pair(profile_ref, live_precision(count_ref, precision_ref) * seen_ref[...], pair_ref)
    spread_rows(matrix_ref, pair_ref, out_ref)


def observe_norm_kernel(
    count_ref, received_ref, precision_ref, profile_ref, matrix_ref, first_ref, second_ref,
    out_ref, turned_ref, seen_ref,
):
    observe(received_ref, matrix_ref, profile_ref, turned_ref, seen_ref)
    seen = seen_ref[...]
    lane = lax.broadcasted_iota(jnp.int32, out_ref.shape, 1)
    parts = (first_ref[0], second_ref[0], second_ref[1], live_precision(count_ref, precision_ref) * seen * seen)
    row = jnp.zeros(out_ref.shape, f32)
    for k in range(4):
        row = jnp.where(lane == k, jnp.sum(parts[k]), row)
    out_ref[...] = row


def split_pair(arrived_ref, pair_ref):
    slots, levels = arrived_ref.shape

    def one(index, carry):
        base = pl.multiple_of(index * CHUNK, CHUNK)
        high, low = halves(arrived_ref[pl.ds(base, CHUNK), :])
        pair_ref[pl.ds(base, CHUNK), :levels] = high
        pair_ref[pl.ds(base, CHUNK), levels:] = low
        return carry

    lax.fori_loop(0, slots // CHUNK, one, 0)


def place_first_kernel(send_ref, arrived_ref, out_ref, matrix_ref, pair_ref):
    slots, levels = arrived_ref.shape
    split_pair(arrived_ref, pair_ref)
    size = 128

    def one(index, carry):
        base = pl.multiple_of(index * size, size)
        column = base + lax.broadcasted_iota(jnp.int32, (size, slots), 0)
        matrix = jnp.where(column == send_ref[...], 1.0, 0.0).astype(bf16)
        matrix_ref[pl.ds(base, size), :] = matrix
        both = mm(matrix, pair_ref[...])
        out_ref[pl.ds(base, size), :] = both[:, :levels] + both[:, levels:]
        return carry

    lax.fori_loop(0, out_ref.shape[0] // size, one, 0)


def place_kernel(matrix_ref, arrived_ref, out_ref, pair_ref):
    levels = arrived_ref.shape[1]
    split_pair(arrived_ref, pair_ref)
    both = mm(matrix_ref[...], pair_ref[...])
    out_ref[...] = both[:, :levels] + both[:, levels:]


def strip_kernel(place_ref, cells_ref, one_ref, two_ref, first_ref, second_ref):
    across, along, _ = cells_ref.shape
    odd = place_ref[1]
    head_or_tail = pl.multiple_of((1 - odd) * (along - HALO), HALO)
    tail_or_head = pl.multiple_of(odd * (along - HALO), HALO)
    for target, at in ((first_ref, head_or_tail), (second_ref, tail_or_head)):
        for k, source in enumerate((one_ref, cells_ref, two_ref)):
            target[k * across : (k + 1) * across] = source[:, pl.ds(at, HALO), :]


def fill(place_ref, target, cells_ref, one_ref, two_ref, first_ref, second_ref):
    across, along, _ = cells_ref.shape
    odd_x, odd_y = place_ref[0], place_ref[1]
    above = (1 - odd_x) * (across + HALO)
    below = odd_x * (across + HALO)
    target[HALO : HALO + across, HALO : HALO + along] = cells_ref[...]
    target[pl.ds(above, HALO), HALO : HALO + along] = one_ref[...]
    target[pl.ds(below, HALO), HALO : HALO + along] = two_ref[...]
    for source, at in ((first_ref, 1 - odd_y), (second_ref, odd_y)):
        start = pl.multiple_of(at * (along + HALO), HALO)
        for k, row in enumerate((above, HALO, below)):
            target[pl.ds(row, HALO), pl.ds(start, HALO), :] = source[k * across : (k + 1) * across]


def conduct_kernel(place_ref, cells_ref, one_ref, two_ref, first_ref, second_ref, east_ref, north_ref, field):
    wide, tall, levels = field.shape
    across, along, _ = cells_ref.shape
    fill(place_ref, field, cells_ref, one_ref, two_ref, first_ref, second_ref)
    edges = (place_ref[2] == 0, place_ref[2] == place_ref[4] - 1, place_ref[3] == 0, place_ref[3] == place_ref[5] - 1)

    @pl.when(edges[0])
    def _():
        field[:HALO] = jnp.zeros((HALO, tall, levels), f32)

    @pl.when(edges[1])
    def _():
        field[HALO + across :] = jnp.zeros((HALO, tall, levels), f32)

    @pl.when(edges[2])
    def _():
        field[:, :HALO] = jnp.zeros((wide, HALO, levels), f32)

    @pl.when(edges[3])
    def _():
        field[:, HALO + along :] = jnp.zeros((wide, HALO, levels), f32)

    def one(i, carry):
        here = COUPLING * field[i]
        after = field[jnp.minimum(i + 1, wide - 1)]
        east_ref[i] = here * after
        north_ref[i, : tall - 1] = here[: tall - 1] * field[i, 1:]
        north_ref[i, tall - 1 :] = jnp.zeros((1, levels), f32)
        return carry

    lax.fori_loop(0, wide, one, 0)


def select_kernel(send_ref, out_ref):
    slots, columns = out_ref.shape
    size = 128
    lane = lax.broadcasted_iota(jnp.int32, (size, size), 1).astype(f32)

    def one(index, carry):
        base = pl.multiple_of(index * size, size)
        wanted = jnp.broadcast_to(send_ref[:, pl.ds(base, size)].astype(f32), (size, size)).T
        for at in range(0, columns, size):
            hit = jnp.where(wanted == lane + at, 1.0, 0.0)
            out_ref[pl.ds(base, size), at : at + size] = hit.astype(bf16)
        return carry

    lax.fori_loop(0, slots // size, one, 0)


def smooth_kernel(place_ref, select_ref, cells_ref, one_ref, two_ref, first_ref, second_ref, east, north, *rest):
    *given, half_ref, full_ref, out_ref, sums_ref, field = rest
    across, along, levels = cells_ref.shape
    wide, tall = across + 2 * HALO, along + 2 * HALO
    fill(place_ref, field, cells_ref, one_ref, two_ref, first_ref, second_ref)

    def sweep(k):
        def row(i, carry):
            here, inward = carry
            after = field[i + 1]
            outward = east[i] * (after - here)
            above = north[i] * (pltpu.roll(here, tall - 1, 0) - here)
            field[i] = here + ((outward - inward) + (above - pltpu.roll(above, 1, 0)))
            return after, outward

        here = field[k]
        lax.fori_loop(k, wide - k, row, (here, east[k - 1] * (here - field[k - 1])), unroll=2)

    def middle():
        return field[HALO : HALO + across, HALO : HALO + along]

    for k in range(1, PASSES + 1):
        sweep(k)
    half = middle()
    half_ref[...] = half
    if given:
        sums_ref[0] = jnp.sum((given[0][...] * half).reshape(-1, 8, levels), axis=0)
        sums_ref[1] = jnp.sum((half * half).reshape(-1, 8, levels), axis=0)
    else:
        sums_ref[0] = jnp.sum((half * half).reshape(-1, 8, levels), axis=0)
    for k in range(PASSES + 1, HALO + 1):
        sweep(k)
    full = middle()
    full_ref[...] = full
    columns = across * along
    pair = jnp.concatenate(halves(full.reshape(columns, levels)), axis=1)

    size = 4 * CHUNK

    def gather(index, carry):
        base = pl.multiple_of(index * size, size)
        both = mm(select_ref[pl.ds(base, size), :], pair)
        out_ref[pl.ds(base, size), :] = both[:, :levels] + both[:, levels:]
        return carry

    lax.fori_loop(0, out_ref.shape[0] // size, gather, 0)


def finish_kernel(sums_ref, b_ref, sb_ref, p_ref, sp_ref, control_ref, increment_ref):
    total = jnp.sum(sums_ref[...], axis=0, keepdims=True)
    lane = lax.broadcasted_iota(jnp.int32, total.shape, 1)
    a, c, e, f = [jnp.sum(jnp.where(lane == k, total, 0.0), axis=1, keepdims=True) for k in range(4)]
    slope = c / a
    first = 1.0 / (1.0 + slope)
    rest = e / a - slope * slope
    ratio = first * first * rest
    curved = rest + (f / a - 2.0 * slope * (e / a) + slope * slope * slope)
    second = ratio / (first * first * curved - ratio * ratio * (1.0 + slope))
    of_b = first + second * (ratio + first * slope)
    of_p = -second * first
    control_ref[...] = of_b * b_ref[...] + of_p * p_ref[...]
    increment_ref[...] = of_b * sb_ref[...] + of_p * sp_ref[...]


def swap(cells, axis, odd):
    count = lax.axis_size(axis)
    pairs = [(i, (i + 1) % count) for i in range(odd, count, 2)]
    return lax.ppermute(cells, axis, pairs + [(j, i) for i, j in pairs])


def exchange(rows):
    return lax.all_to_all(rows, ("gx", "gy"), split_axis=0, concat_axis=0, tiled=True)


def params(mib):
    return pltpu.CompilerParams(vmem_limit_bytes=mib * MIB)


def cost(flops, size):
    return pl.CostEstimate(flops=flops, bytes_accessed=size, transcendentals=0)


def on_device(
    length_scale, innovation, observed_precision, profile_weight, stencil_weight, send_rows, stencil_rows, obs_count,
):
    across, along, levels = length_scale.shape
    owners, slot_count = send_rows.shape[1:]
    slots = owners * slot_count
    columns = across * along
    obs = innovation.shape[0]
    send = send_rows.reshape(1, slots)
    innovation = innovation.reshape(1, obs)
    precision = observed_precision.reshape(1, obs)
    at_x, at_y = lax.axis_index("gx"), lax.axis_index("gy")
    sizes = [jnp.int32(lax.axis_size(axis)) for axis in ("gx", "gy")]
    place = jnp.stack([at_x % 2, at_y % 2, at_x, at_y, *sizes]).astype(jnp.int32)

    whole = pl.BlockSpec(memory_space=pltpu.VMEM)
    scalar = pl.BlockSpec(memory_space=pltpu.SMEM)
    afar = pl.BlockSpec(memory_space=pltpu.HBM)
    slot_rows = jax.ShapeDtypeStruct((slots, levels), f32)
    tile = jax.ShapeDtypeStruct((across, along, levels), f32)
    strip = jax.ShapeDtypeStruct((across + 2 * HALO, HALO, levels), f32)
    grown = (across + 2 * HALO, along + 2 * HALO, levels)
    pair_scratch = pltpu.VMEM((2 * obs, 2 * levels), bf16)
    turned_scratch = pltpu.VMEM((2 * levels, slots), bf16)
    seen_scratch = pltpu.VMEM((1, obs), f32)

    def trade(rows):
        return exchange(rows.reshape(owners, slot_count, levels)).reshape(slots, levels)

    def strips(cells, one, two):
        return pl.pallas_call(
            strip_kernel,
            out_shape=(strip, strip),
            in_specs=[scalar] + [whole] * 3,
            out_specs=(whole, whole),
            compiler_params=params(2),
            name="strips",
        )(place, cells, one, two)

    def over_x(cells):
        return swap(cells, "gx", 0), swap(cells, "gx", 1)

    def over_y(first, second):
        return swap(first, "gy", 0), swap(second, "gy", 1)

    scale_x = over_x(length_scale)
    stencil_rows, send, place = lax.optimization_barrier((stencil_rows, send, place))
    matrix = pl.pallas_call(
        matrix_kernel,
        out_shape=jax.ShapeDtypeStruct((slots, 2 * obs), bf16),
        in_specs=[afar, afar],
        out_specs=whole,
        scratch_shapes=[
            pltpu.VMEM((4, obs), jnp.int32),
            pltpu.VMEM((4, obs), f32),
            pltpu.SemaphoreType.DMA((2,)),
        ],
        compiler_params=params(4),
        cost_estimate=cost(1 << 30, 1 << 24),
        name="matrix",
    )(*(pltpu.with_memory_space_constraint(x, pltpu.HBM) for x in (stencil_rows, stencil_weight)))
    innovation, *scale_x = lax.optimization_barrier((innovation, *scale_x))
    spread = pl.pallas_call(
        spread_kernel,
        out_shape=slot_rows,
        in_specs=[scalar] + [whole] * 4,
        out_specs=whole,
        scratch_shapes=[pair_scratch],
        compiler_params=params(14),
        cost_estimate=cost(8 << 30, 1 << 24),
        name="spread",
    )(obs_count, innovation, precision, profile_weight, matrix)
    spread, send = lax.optimization_barrier((spread, send))
    arrived, send, *scale_x = lax.optimization_barrier((trade(spread), send, *scale_x))

    cells, placing = pl.pallas_call(
        place_first_kernel,
        out_shape=(jax.ShapeDtypeStruct((columns, levels), f32), jax.ShapeDtypeStruct((columns, slots), bf16)),
        in_specs=[whole, whole],
        out_specs=(whole, whole),
        scratch_shapes=[pltpu.VMEM((slots, 2 * levels), bf16)],
        compiler_params=params(8),
        name="place_first",
    )(send, arrived)
    selecting = pl.pallas_call(
        select_kernel,
        out_shape=jax.ShapeDtypeStruct((slots, columns), bf16),
        in_specs=[whole],
        out_specs=whole,
        compiler_params=params(2),
        cost_estimate=cost(1 << 28, 1 << 22),
        name="select",
    )(send)
    scale_y = over_y(*strips(length_scale, *scale_x))
    conductances = pl.pallas_call(
        conduct_kernel,
        out_shape=(jax.ShapeDtypeStruct(grown, f32),) * 2,
        in_specs=[scalar] + [whole] * 5,
        out_specs=(whole, whole),
        scratch_shapes=[pltpu.VMEM(grown, f32)],
        compiler_params=params(4),
        cost_estimate=cost(1 << 26, 1 << 22),
        name="conduct",
    )(place, length_scale, *scale_x, *scale_y)

    def smooth_twice(cells, given):
        cells = cells.reshape(across, along, levels)
        aside = over_x(cells)
        count = 1 + len(given)
        return pl.pallas_call(
            smooth_kernel,
            out_shape=(tile, tile, slot_rows, jax.ShapeDtypeStruct((count, 8, levels), f32)),
            in_specs=[scalar] + [whole] * (8 + len(given)),
            out_specs=(whole,) * 4,
            scratch_shapes=[pltpu.VMEM(grown, f32)],
            compiler_params=params(10),
            name="smooth",
        )(place, selecting, cells, *aside, *over_y(*strips(cells, *aside)), *conductances, *given)

    b, sb, outgoing, first_sums = smooth_twice(cells, ())

    spread = pl.pallas_call(
        observe_adjoint_kernel,
        out_shape=slot_rows,
        in_specs=[scalar] + [whole] * 4,
        out_specs=whole,
        scratch_shapes=[turned_scratch, seen_scratch, pair_scratch],
        compiler_params=params(16),
        name="observe_adjoint",
    )(obs_count, trade(outgoing), precision, profile_weight, matrix)

    cells = pl.pallas_call(
        place_kernel,
        out_shape=jax.ShapeDtypeStruct((columns, levels), f32),
        in_specs=[whole, whole],
        out_specs=whole,
        scratch_shapes=[pltpu.VMEM((slots, 2 * levels), bf16)],
        compiler_params=params(8),
        name="place",
    )(placing, trade(spread))
    p, sp, outgoing, second_sums = smooth_twice(cells, (b,))

    sums = pl.pallas_call(
        observe_norm_kernel,
        out_shape=jax.ShapeDtypeStruct((owners, levels), f32),
        in_specs=[scalar] + [whole] * 6,
        out_specs=whole,
        scratch_shapes=[turned_scratch, seen_scratch],
        compiler_params=params(14),
        name="observe_norm",
    )(obs_count, trade(outgoing), precision, profile_weight, matrix, first_sums, second_sums)

    sums = exchange(sums.reshape(owners, 1, levels)).reshape(owners, levels)

    return pl.pallas_call(
        finish_kernel,
        out_shape=(
            jax.ShapeDtypeStruct((columns, levels), f32),
            jax.ShapeDtypeStruct((columns, levels), f32),
        ),
        in_specs=[whole] * 5,
        out_specs=(whole, whole),
        compiler_params=params(4),
        name="finish",
    )(sums, *(x.reshape(columns, levels) for x in (b, sb, p, sp)))


def solution(mesh):
    def run(*args):
        control, increment = on_device(*args)
        shape = args[0].shape
        return control.reshape(shape), increment.reshape(shape)

    return jax.shard_map(
        run,
        mesh=mesh,
        in_specs=(
            P("gx", "gy", None),
            P(("gx", "gy")),
            P(("gx", "gy")),
            P(("gx", "gy"), None),
            P(None, ("gx", "gy")),
            P(("gx", "gy"), None, None),
            P(None, ("gx", "gy")),
            P(("gx", "gy")),
        ),
        out_specs=(P("gx", "gy", None), P("gx", "gy", None)),
        check_vma=False,
    )
```

```python
import functools

import jax
import jax.numpy as jnp
from jax import lax
from jax.experimental import pallas as pl
from jax.experimental.pallas import tpu as pltpu
from jax.sharding import PartitionSpec as P


MIB = 1 << 20
COUPLING = 0.12
PASSES = 4
HALO = 2 * PASSES
CHUNK = 256
bf16 = jnp.bfloat16
f32 = jnp.float32


def mm(lhs, rhs):
    return jnp.dot(lhs, rhs, preferred_element_type=f32)


def halves(values):
    high = values.astype(bf16)
    return high, (values - high.astype(f32)).astype(bf16)


def live_precision(count_ref, precision_ref):
    place = lax.broadcasted_iota(jnp.int32, precision_ref.shape, 1)
    return jnp.where(place < count_ref[0], precision_ref[...], 0.0)


def merge_repeats(rows_ref, weights_ref):
    rows = [rows_ref[k : k + 1, :] for k in range(4)]
    weights = [weights_ref[k : k + 1, :] for k in range(4)]
    for k in range(1, 4):
        for j in range(k):
            same = rows[k] == rows[j]
            weights[j] = weights[j] + jnp.where(same, weights[k], 0.0)
            weights[k] = jnp.where(same, 0.0, weights[k])
    return rows, [halves(weight) for weight in weights]


def flatten_send(send_ref, out_ref):
    _, slot_count, owners = send_ref.shape
    lanes = 128
    group = lanes // slot_count
    wide = lax.broadcasted_iota(jnp.int32, (slot_count, lanes), 1)
    tall = lax.broadcasted_iota(jnp.int32, (slot_count, lanes), 0)
    again = jnp.where(lax.rem(wide, slot_count) == tall, 1.0, 0.0)
    repeated = jnp.dot(
        send_ref[0].astype(f32).T, again, precision=lax.Precision.HIGHEST, preferred_element_type=f32
    )
    owner = lax.broadcasted_iota(jnp.int32, (owners, lanes), 0)
    lane = lax.broadcasted_iota(jnp.int32, (owners, lanes), 1)
    kept = jnp.where(lax.div(lane, slot_count) == lax.rem(owner, group), repeated, 0.0)
    lines = jnp.sum(kept.reshape(owners // group, group, lanes), axis=1).astype(jnp.int32)
    for k in range(owners // group):
        out_ref[:, k * lanes : (k + 1) * lanes] = lines[k : k + 1]


def spread_first_kernel(
    count_ref, rows_hbm, weights_hbm, send_hbm, innovation_hbm, precision_hbm, profile_hbm,
    matrix_ref, out_ref, flat_ref,
    rows_ref, weights_ref, send_ref, innovation_ref, precision_ref, profile_ref, pair_ref, sems,
):
    moves = (
        (rows_hbm, rows_ref), (weights_hbm, weights_ref), (send_hbm, send_ref),
        (innovation_hbm, innovation_ref), (precision_hbm, precision_ref), (profile_hbm, profile_ref),
    )
    copies = [pltpu.make_async_copy(*move, sems.at[k]) for k, move in enumerate(moves)]
    for copy in copies:
        copy.start()
    for copy in copies[:5]:
        copy.wait()
    flatten_send(send_ref, flat_ref)
    rows, parts = merge_repeats(rows_ref, weights_ref)
    forcing = live_precision(count_ref, precision_ref) * innovation_ref[...]
    copies[5].wait()
    fill_pair(profile_ref, forcing, pair_ref)
    slots, obs, levels = matrix_ref.shape[0], rows_ref.shape[1], out_ref.shape[1]
    shape = (CHUNK, CHUNK)
    slot = lax.broadcasted_iota(jnp.int32, shape, 0).astype(f32).astype(bf16)

    def one(index, carry):
        base = pl.multiple_of(index * CHUNK, CHUNK)
        near = [(row - base).astype(f32).astype(bf16) for row in rows]
        for at in range(0, obs, CHUNK):
            high = jnp.zeros(shape, bf16)
            low = jnp.zeros(shape, bf16)
            for k in (3, 2, 1, 0):
                cut = slice(at, at + CHUNK)
                hit = jnp.broadcast_to(near[k][:, cut], shape) == slot
                high = jnp.where(hit, jnp.broadcast_to(parts[k][0][:, cut], shape), high)
                low = jnp.where(hit, jnp.broadcast_to(parts[k][1][:, cut], shape), low)
            matrix_ref[pl.ds(base, CHUNK), at : at + CHUNK] = high
            matrix_ref[pl.ds(base, CHUNK), obs + at : obs + at + CHUNK] = low
        both = mm(matrix_ref[pl.ds(base, CHUNK), :], pair_ref[...])
        out_ref[pl.ds(base, CHUNK), :] = both[:, :levels] + both[:, levels:]
        return carry

    lax.fori_loop(0, slots // CHUNK, one, 0)


def spread_rows(matrix_ref, pair_ref, out_ref):
    levels = out_ref.shape[1]
    size = 4 * CHUNK

    def one(index, carry):
        base = pl.multiple_of(index * size, size)
        both = mm(matrix_ref[pl.ds(base, size), :], pair_ref[...])
        out_ref[pl.ds(base, size), :] = both[:, :levels] + both[:, levels:]
        return carry

    lax.fori_loop(0, out_ref.shape[0] // size, one, 0)


def fill_pair(profile_ref, forcing, pair_ref):
    obs, levels = profile_ref.shape
    for at in range(0, obs, levels):
        column = jnp.broadcast_to(forcing[:, at : at + levels], (levels, levels)).T
        high, low = halves(profile_ref[at : at + levels, :] * column)
        for base in (at, obs + at):
            pair_ref[base : base + levels, :levels] = high
            pair_ref[base : base + levels, levels:] = low


def observe(received_ref, matrix_ref, profile_ref, turned_ref, seen_ref):
    slots, levels = received_ref.shape
    obs = profile_ref.shape[0]
    for at in range(0, slots, levels):
        high, low = halves(received_ref[at : at + levels, :].T)
        turned_ref[:levels, at : at + levels] = high
        turned_ref[levels:, at : at + levels] = low
    size = 4 * CHUNK

    def one(index, carry):
        base = pl.multiple_of(index * size, size)
        both = mm(turned_ref[...], matrix_ref[:, pl.ds(base, size)])
        gathered = both[:levels] + both[levels:]
        gathered = gathered + mm(
            turned_ref[:levels], matrix_ref[:, pl.ds(pl.multiple_of(obs + index * size, size), size)]
        )
        seen_ref[:, pl.ds(base, size)] = jnp.sum(
            profile_ref[pl.ds(base, size), :].T * gathered, axis=0, keepdims=True
        )
        return carry

    lax.fori_loop(0, obs // size, one, 0)


def observe_adjoint_kernel(
    count_ref, received_ref, precision_ref, profile_ref, matrix_ref, out_ref, turned_ref, seen_ref, pair_ref,
):
    observe(received_ref, matrix_ref, profile_ref, turned_ref, seen_ref)
    fill_pair(profile_ref, live_precision(count_ref, precision_ref) * seen_ref[...], pair_ref)
    spread_rows(matrix_ref, pair_ref, out_ref)


def observe_norm_kernel(
    count_ref, received_ref, precision_ref, profile_ref, matrix_ref, first_ref, second_ref,
    out_ref, turned_ref, seen_ref,
):
    observe(received_ref, matrix_ref, profile_ref, turned_ref, seen_ref)
    seen = seen_ref[...]
    lane = lax.broadcasted_iota(jnp.int32, out_ref.shape, 1)
    parts = (first_ref[0], second_ref[0], second_ref[1], live_precision(count_ref, precision_ref) * seen * seen)
    row = jnp.zeros(out_ref.shape, f32)
    for k in range(4):
        row = jnp.where(lane == k, jnp.sum(parts[k]), row)
    out_ref[...] = row


def split_pair(arrived_ref, pair_ref):
    slots, levels = arrived_ref.shape

    def one(index, carry):
        base = pl.multiple_of(index * CHUNK, CHUNK)
        high, low = halves(arrived_ref[pl.ds(base, CHUNK), :])
        pair_ref[pl.ds(base, CHUNK), :levels] = high
        pair_ref[pl.ds(base, CHUNK), levels:] = low
        return carry

    lax.fori_loop(0, slots // CHUNK, one, 0)


def place_first_kernel(send_ref, arrived_ref, out_ref, matrix_ref, pair_ref):
    slots, levels = arrived_ref.shape
    split_pair(arrived_ref, pair_ref)
    size = 128

    def one(index, carry):
        base = pl.multiple_of(index * size, size)
        column = base + lax.broadcasted_iota(jnp.int32, (size, slots), 0)
        matrix = jnp.where(column == send_ref[...], 1.0, 0.0).astype(bf16)
        matrix_ref[pl.ds(base, size), :] = matrix
        both = mm(matrix, pair_ref[...])
        out_ref[pl.ds(base, size), :] = both[:, :levels] + both[:, levels:]
        return carry

    lax.fori_loop(0, out_ref.shape[0] // size, one, 0)


def place_kernel(matrix_ref, arrived_ref, out_ref, pair_ref):
    levels = arrived_ref.shape[1]
    split_pair(arrived_ref, pair_ref)
    both = mm(matrix_ref[...], pair_ref[...])
    out_ref[...] = both[:, :levels] + both[:, levels:]


def spot(place_ref, sizes):
    return lax.div(place_ref[0], sizes[1]), lax.rem(place_ref[0], sizes[1])


def strip_kernel(sizes, place_ref, cells_ref, one_ref, two_ref, first_ref, second_ref):
    across, along, _ = cells_ref.shape
    odd = lax.rem(spot(place_ref, sizes)[1], 2)
    head_or_tail = pl.multiple_of((1 - odd) * (along - HALO), HALO)
    tail_or_head = pl.multiple_of(odd * (along - HALO), HALO)
    for target, at in ((first_ref, head_or_tail), (second_ref, tail_or_head)):
        for k, source in enumerate((one_ref, cells_ref, two_ref)):
            target[k * across : (k + 1) * across] = source[:, pl.ds(at, HALO), :]


def fill(at_x, at_y, target, cells_ref, one_ref, two_ref, first_ref, second_ref):
    across, along, _ = cells_ref.shape
    odd_x, odd_y = lax.rem(at_x, 2), lax.rem(at_y, 2)
    above = (1 - odd_x) * (across + HALO)
    below = odd_x * (across + HALO)
    target[HALO : HALO + across, HALO : HALO + along] = cells_ref[...]
    target[pl.ds(above, HALO), HALO : HALO + along] = one_ref[...]
    target[pl.ds(below, HALO), HALO : HALO + along] = two_ref[...]
    for source, at in ((first_ref, 1 - odd_y), (second_ref, odd_y)):
        start = pl.multiple_of(at * (along + HALO), HALO)
        for k, row in enumerate((above, HALO, below)):
            target[pl.ds(row, HALO), pl.ds(start, HALO), :] = source[k * across : (k + 1) * across]


def conduct_kernel(sizes, place_ref, cells_ref, one_ref, two_ref, first_ref, second_ref, east_ref, north_ref, field):
    wide, tall, levels = field.shape
    across, along, _ = cells_ref.shape
    at_x, at_y = spot(place_ref, sizes)
    fill(at_x, at_y, field, cells_ref, one_ref, two_ref, first_ref, second_ref)
    edges = (at_x == 0, at_x == sizes[0] - 1, at_y == 0, at_y == sizes[1] - 1)

    @pl.when(edges[0])
    def _():
        field[:HALO] = jnp.zeros((HALO, tall, levels), f32)

    @pl.when(edges[1])
    def _():
        field[HALO + across :] = jnp.zeros((HALO, tall, levels), f32)

    @pl.when(edges[2])
    def _():
        field[:, :HALO] = jnp.zeros((wide, HALO, levels), f32)

    @pl.when(edges[3])
    def _():
        field[:, HALO + along :] = jnp.zeros((wide, HALO, levels), f32)

    def one(i, carry):
        here = COUPLING * field[i]
        after = field[jnp.minimum(i + 1, wide - 1)]
        east_ref[i] = here * after
        north_ref[i, : tall - 1] = here[: tall - 1] * field[i, 1:]
        north_ref[i, tall - 1 :] = jnp.zeros((1, levels), f32)
        return carry

    lax.fori_loop(0, wide, one, 0)


def select_kernel(send_ref, out_ref):
    slots, columns = out_ref.shape
    size = 128
    lane = lax.broadcasted_iota(jnp.int32, (size, size), 1).astype(f32)

    def one(index, carry):
        base = pl.multiple_of(index * size, size)
        wanted = jnp.broadcast_to(send_ref[:, pl.ds(base, size)].astype(f32), (size, size)).T
        for at in range(0, columns, size):
            hit = jnp.where(wanted == lane + at, 1.0, 0.0)
            out_ref[pl.ds(base, size), at : at + size] = hit.astype(bf16)
        return carry

    lax.fori_loop(0, slots // size, one, 0)


def smooth_kernel(sizes, place_ref, select_ref, cells_ref, one_ref, two_ref, first_ref, second_ref, east, north, *rest):
    *given, half_ref, full_ref, out_ref, sums_ref, field = rest
    across, along, levels = cells_ref.shape
    wide, tall = across + 2 * HALO, along + 2 * HALO
    fill(*spot(place_ref, sizes), field, cells_ref, one_ref, two_ref, first_ref, second_ref)

    def sweep(k):
        def row(i, carry):
            here, inward = carry
            after = field[i + 1]
            outward = east[i] * (after - here)
            above = north[i] * (pltpu.roll(here, tall - 1, 0) - here)
            field[i] = here + ((outward - inward) + (above - pltpu.roll(above, 1, 0)))
            return after, outward

        here = field[k]
        lax.fori_loop(k, wide - k, row, (here, east[k - 1] * (here - field[k - 1])), unroll=2)

    def middle():
        return field[HALO : HALO + across, HALO : HALO + along]

    for k in range(1, PASSES + 1):
        sweep(k)
    half = middle()
    half_ref[...] = half
    if given:
        sums_ref[0] = jnp.sum((given[0][...] * half).reshape(-1, 8, levels), axis=0)
        sums_ref[1] = jnp.sum((half * half).reshape(-1, 8, levels), axis=0)
    else:
        sums_ref[0] = jnp.sum((half * half).reshape(-1, 8, levels), axis=0)
    for k in range(PASSES + 1, HALO + 1):
        sweep(k)
    full = middle()
    full_ref[...] = full
    columns = across * along
    pair = jnp.concatenate(halves(full.reshape(columns, levels)), axis=1)

    size = 4 * CHUNK

    def gather(index, carry):
        base = pl.multiple_of(index * size, size)
        both = mm(select_ref[pl.ds(base, size), :], pair)
        out_ref[pl.ds(base, size), :] = both[:, :levels] + both[:, levels:]
        return carry

    lax.fori_loop(0, out_ref.shape[0] // size, gather, 0)


def finish_kernel(sums_ref, b_ref, sb_ref, p_ref, sp_ref, control_ref, increment_ref):
    total = jnp.sum(sums_ref[...], axis=0, keepdims=True)
    lane = lax.broadcasted_iota(jnp.int32, total.shape, 1)
    a, c, e, f = [jnp.sum(jnp.where(lane == k, total, 0.0), axis=1, keepdims=True) for k in range(4)]
    slope = c / a
    first = 1.0 / (1.0 + slope)
    rest = e / a - slope * slope
    ratio = first * first * rest
    curved = rest + (f / a - 2.0 * slope * (e / a) + slope * slope * slope)
    second = ratio / (first * first * curved - ratio * ratio * (1.0 + slope))
    of_b = first + second * (ratio + first * slope)
    of_p = -second * first
    control_ref[...] = of_b * b_ref[...] + of_p * p_ref[...]
    increment_ref[...] = of_b * sb_ref[...] + of_p * sp_ref[...]


def swap(cells, axis, odd):
    count = lax.axis_size(axis)
    pairs = [(i, (i + 1) % count) for i in range(odd, count, 2)]
    return lax.ppermute(cells, axis, pairs + [(j, i) for i, j in pairs])


def exchange(rows):
    return lax.all_to_all(rows, ("gx", "gy"), split_axis=0, concat_axis=0, tiled=True)


def params(mib):
    return pltpu.CompilerParams(vmem_limit_bytes=mib * MIB)


def cost(flops, size):
    return pl.CostEstimate(flops=flops, bytes_accessed=size, transcendentals=0)


def on_device(
    length_scale, innovation, observed_precision, profile_weight, stencil_weight, send_rows, stencil_rows, obs_count,
):
    across, along, levels = length_scale.shape
    owners, slot_count = send_rows.shape[1:]
    slots = owners * slot_count
    columns = across * along
    obs = innovation.shape[0]
    innovation = innovation.reshape(1, obs)
    precision = observed_precision.reshape(1, obs)
    sizes = tuple(lax.axis_size(axis) for axis in ("gx", "gy"))
    place = lax.axis_index(("gx", "gy")).astype(jnp.int32).reshape(1)

    whole = pl.BlockSpec(memory_space=pltpu.VMEM)
    scalar = pl.BlockSpec(memory_space=pltpu.SMEM)
    afar = pl.BlockSpec(memory_space=pltpu.HBM)
    slot_rows = jax.ShapeDtypeStruct((slots, levels), f32)
    tile = jax.ShapeDtypeStruct((across, along, levels), f32)
    strip = jax.ShapeDtypeStruct((across + 2 * HALO, HALO, levels), f32)
    grown = (across + 2 * HALO, along + 2 * HALO, levels)
    pair_scratch = pltpu.VMEM((2 * obs, 2 * levels), bf16)
    turned_scratch = pltpu.VMEM((2 * levels, slots), bf16)
    seen_scratch = pltpu.VMEM((1, obs), f32)

    def trade(rows):
        return exchange(rows.reshape(owners, slot_count, levels)).reshape(slots, levels)

    def strips(cells, one, two):
        return pl.pallas_call(
            functools.partial(strip_kernel, sizes),
            out_shape=(strip, strip),
            in_specs=[scalar] + [whole] * 3,
            out_specs=(whole, whole),
            compiler_params=params(2),
            name="strips",
        )(place, cells, one, two)

    def over_x(cells):
        return swap(cells, "gx", 0), swap(cells, "gx", 1)

    def over_y(first, second):
        return swap(first, "gy", 0), swap(second, "gy", 1)

    scale_x = over_x(length_scale)
    stencil_rows, place = lax.optimization_barrier((stencil_rows, place))
    turned = send_rows.transpose(0, 2, 1)
    given = (stencil_rows, stencil_weight, turned, innovation, precision, profile_weight)
    matrix, spread, send = pl.pallas_call(
        spread_first_kernel,
        out_shape=(
            jax.ShapeDtypeStruct((slots, 2 * obs), bf16),
            slot_rows,
            jax.ShapeDtypeStruct((1, slots), jnp.int32),
        ),
        in_specs=[scalar] + [afar] * 6,
        out_specs=(whole,) * 3,
        scratch_shapes=[
            *(pltpu.VMEM(x.shape, x.dtype) for x in given),
            pair_scratch,
            pltpu.SemaphoreType.DMA((6,)),
        ],
        compiler_params=params(14),
        cost_estimate=cost(8 << 30, 1 << 24),
        name="spread_first",
    )(obs_count, *(pltpu.with_memory_space_constraint(x, pltpu.HBM) for x in given))
    spread, *scale_x = lax.optimization_barrier((spread, *scale_x))
    arrived, send, *scale_x = lax.optimization_barrier((trade(spread), send, *scale_x))

    cells, placing = pl.pallas_call(
        place_first_kernel,
        out_shape=(jax.ShapeDtypeStruct((columns, levels), f32), jax.ShapeDtypeStruct((columns, slots), bf16)),
        in_specs=[whole, whole],
        out_specs=(whole, whole),
        scratch_shapes=[pltpu.VMEM((slots, 2 * levels), bf16)],
        compiler_params=params(8),
        name="place_first",
    )(send, arrived)
    selecting = pl.pallas_call(
        select_kernel,
        out_shape=jax.ShapeDtypeStruct((slots, columns), bf16),
        in_specs=[whole],
        out_specs=whole,
        compiler_params=params(2),
        cost_estimate=cost(1 << 28, 1 << 22),
        name="select",
    )(send)
    scale_y = over_y(*strips(length_scale, *scale_x))
    conductances = pl.pallas_call(
        functools.partial(conduct_kernel, sizes),
        out_shape=(jax.ShapeDtypeStruct(grown, f32),) * 2,
        in_specs=[scalar] + [whole] * 5,
        out_specs=(whole, whole),
        scratch_shapes=[pltpu.VMEM(grown, f32)],
        compiler_params=params(4),
        cost_estimate=cost(1 << 26, 1 << 22),
        name="conduct",
    )(place, length_scale, *scale_x, *scale_y)

    def smooth_twice(cells, given):
        cells = cells.reshape(across, along, levels)
        aside = over_x(cells)
        count = 1 + len(given)
        return pl.pallas_call(
            functools.partial(smooth_kernel, sizes),
            out_shape=(tile, tile, slot_rows, jax.ShapeDtypeStruct((count, 8, levels), f32)),
            in_specs=[scalar] + [whole] * (8 + len(given)),
            out_specs=(whole,) * 4,
            scratch_shapes=[pltpu.VMEM(grown, f32)],
            compiler_params=params(10),
            name="smooth",
        )(place, selecting, cells, *aside, *over_y(*strips(cells, *aside)), *conductances, *given)

    b, sb, outgoing, first_sums = smooth_twice(cells, ())

    spread = pl.pallas_call(
        observe_adjoint_kernel,
        out_shape=slot_rows,
        in_specs=[scalar] + [whole] * 4,
        out_specs=whole,
        scratch_shapes=[turned_scratch, seen_scratch, pair_scratch],
        compiler_params=params(16),
        name="observe_adjoint",
    )(obs_count, trade(outgoing), precision, profile_weight, matrix)

    cells = pl.pallas_call(
        place_kernel,
        out_shape=jax.ShapeDtypeStruct((columns, levels), f32),
        in_specs=[whole, whole],
        out_specs=whole,
        scratch_shapes=[pltpu.VMEM((slots, 2 * levels), bf16)],
        compiler_params=params(8),
        name="place",
    )(placing, trade(spread))
    p, sp, outgoing, second_sums = smooth_twice(cells, (b,))

    sums = pl.pallas_call(
        observe_norm_kernel,
        out_shape=jax.ShapeDtypeStruct((owners, levels), f32),
        in_specs=[scalar] + [whole] * 6,
        out_specs=whole,
        scratch_shapes=[turned_scratch, seen_scratch],
        compiler_params=params(14),
        name="observe_norm",
    )(obs_count, trade(outgoing), precision, profile_weight, matrix, first_sums, second_sums)

    sums = exchange(sums.reshape(owners, 1, levels)).reshape(owners, levels)

    return pl.pallas_call(
        finish_kernel,
        out_shape=(
            jax.ShapeDtypeStruct((columns, levels), f32),
            jax.ShapeDtypeStruct((columns, levels), f32),
        ),
        in_specs=[whole] * 5,
        out_specs=(whole, whole),
        compiler_params=params(4),
        name="finish",
    )(sums, *(x.reshape(columns, levels) for x in (b, sb, p, sp)))


def solution(mesh):
    def run(*args):
        control, increment = on_device(*args)
        shape = args[0].shape
        return control.reshape(shape), increment.reshape(shape)

    return jax.shard_map(
        run,
        mesh=mesh,
        in_specs=(
            P("gx", "gy", None),
            P(("gx", "gy")),
            P(("gx", "gy")),
            P(("gx", "gy"), None),
            P(None, ("gx", "gy")),
            P(("gx", "gy"), None, None),
            P(None, ("gx", "gy")),
            P(("gx", "gy")),
        ),
        out_specs=(P("gx", "gy", None), P("gx", "gy", None)),
        check_vma=False,
    )
```

```python
import functools

import jax
import jax.numpy as jnp
from jax import lax
from jax.experimental import pallas as pl
from jax.experimental.pallas import tpu as pltpu
from jax.sharding import PartitionSpec as P


MIB = 1 << 20
COUPLING = 0.12
PASSES = 4
HALO = 2 * PASSES
CHUNK = 256
bf16 = jnp.bfloat16
f32 = jnp.float32


def mm(lhs, rhs):
    return jnp.dot(lhs, rhs, preferred_element_type=f32)


def halves(values):
    high = values.astype(bf16)
    return high, (values - high.astype(f32)).astype(bf16)


def live_precision(count_ref, precision_ref):
    place = lax.broadcasted_iota(jnp.int32, precision_ref.shape, 1)
    return jnp.where(place < count_ref[0], precision_ref[...], 0.0)


def merge_repeats(rows_ref, weights_ref):
    rows = [rows_ref[k : k + 1, :] for k in range(4)]
    weights = [weights_ref[k : k + 1, :] for k in range(4)]
    for k in range(1, 4):
        for j in range(k):
            same = rows[k] == rows[j]
            weights[j] = weights[j] + jnp.where(same, weights[k], 0.0)
            weights[k] = jnp.where(same, 0.0, weights[k])
    return rows, [halves(weight) for weight in weights]


def flatten_send(send_ref, out_ref):
    _, slot_count, owners = send_ref.shape
    lanes = 128
    group = lanes // slot_count
    wide = lax.broadcasted_iota(jnp.int32, (slot_count, lanes), 1)
    tall = lax.broadcasted_iota(jnp.int32, (slot_count, lanes), 0)
    again = jnp.where(lax.rem(wide, slot_count) == tall, 1.0, 0.0)
    repeated = jnp.dot(
        send_ref[0].astype(f32).T, again, precision=lax.Precision.HIGHEST, preferred_element_type=f32
    )
    owner = lax.broadcasted_iota(jnp.int32, (owners, lanes), 0)
    lane = lax.broadcasted_iota(jnp.int32, (owners, lanes), 1)
    kept = jnp.where(lax.div(lane, slot_count) == lax.rem(owner, group), repeated, 0.0)
    lines = jnp.sum(kept.reshape(owners // group, group, lanes), axis=1).astype(jnp.int32)
    for k in range(owners // group):
        out_ref[:, k * lanes : (k + 1) * lanes] = lines[k : k + 1]


def spread_first_kernel(
    count_ref, rows_hbm, weights_hbm, send_hbm, innovation_hbm, precision_hbm, profile_hbm,
    matrix_ref, out_ref, flat_ref,
    rows_ref, weights_ref, send_ref, innovation_ref, precision_ref, profile_ref, pair_ref, sems,
):
    moves = (
        (rows_hbm, rows_ref), (weights_hbm, weights_ref), (send_hbm, send_ref),
        (innovation_hbm, innovation_ref), (precision_hbm, precision_ref), (profile_hbm, profile_ref),
    )
    copies = [pltpu.make_async_copy(*move, sems.at[k]) for k, move in enumerate(moves)]
    for copy in copies:
        copy.start()
    for copy in copies[:5]:
        copy.wait()
    flatten_send(send_ref, flat_ref)
    rows, parts = merge_repeats(rows_ref, weights_ref)
    forcing = live_precision(count_ref, precision_ref) * innovation_ref[...]
    copies[5].wait()
    fill_pair(profile_ref, forcing, pair_ref)
    slots, obs, levels = matrix_ref.shape[0], rows_ref.shape[1], out_ref.shape[1]
    shape = (CHUNK, CHUNK)
    slot = lax.broadcasted_iota(jnp.int32, shape, 0).astype(f32).astype(bf16)

    def one(index, carry):
        base = pl.multiple_of(index * CHUNK, CHUNK)
        near = [(row - base).astype(f32).astype(bf16) for row in rows]
        for at in range(0, obs, CHUNK):
            high = jnp.zeros(shape, bf16)
            low = jnp.zeros(shape, bf16)
            for k in (3, 2, 1, 0):
                cut = slice(at, at + CHUNK)
                hit = jnp.broadcast_to(near[k][:, cut], shape) == slot
                high = jnp.where(hit, jnp.broadcast_to(parts[k][0][:, cut], shape), high)
                low = jnp.where(hit, jnp.broadcast_to(parts[k][1][:, cut], shape), low)
            matrix_ref[pl.ds(base, CHUNK), at : at + CHUNK] = high
            matrix_ref[pl.ds(base, CHUNK), obs + at : obs + at + CHUNK] = low
        both = mm(matrix_ref[pl.ds(base, CHUNK), :], pair_ref[...])
        out_ref[pl.ds(base, CHUNK), :] = both[:, :levels] + both[:, levels:]
        return carry

    lax.fori_loop(0, slots // CHUNK, one, 0)


def spread_rows(matrix_ref, pair_ref, out_ref):
    slots, levels = out_ref.shape
    size = slots // 2
    for base in range(0, slots, size):
        both = mm(matrix_ref[base : base + size, :], pair_ref[...])
        out_ref[base : base + size, :] = both[:, :levels] + both[:, levels:]


def fill_pair(profile_ref, forcing, pair_ref):
    obs, levels = profile_ref.shape
    for at in range(0, obs, levels):
        column = jnp.broadcast_to(forcing[:, at : at + levels], (levels, levels)).T
        high, low = halves(profile_ref[at : at + levels, :] * column)
        for base in (at, obs + at):
            pair_ref[base : base + levels, :levels] = high
            pair_ref[base : base + levels, levels:] = low


def observe(received_ref, matrix_ref, profile_ref, turned_ref, seen_ref):
    slots, levels = received_ref.shape
    obs = profile_ref.shape[0]
    for at in range(0, slots, levels):
        high, low = halves(received_ref[at : at + levels, :].T)
        turned_ref[:levels, at : at + levels] = high
        turned_ref[levels:, at : at + levels] = low
    size = obs // 2
    for base in range(0, obs, size):
        both = mm(turned_ref[...], matrix_ref[:, base : base + size])
        gathered = both[:levels] + both[levels:]
        gathered = gathered + mm(turned_ref[:levels], matrix_ref[:, obs + base : obs + base + size])
        seen_ref[:, base : base + size] = jnp.sum(
            profile_ref[base : base + size, :].T * gathered, axis=0, keepdims=True
        )


def observe_adjoint_kernel(
    count_ref, received_ref, precision_ref, profile_ref, matrix_ref, out_ref, turned_ref, seen_ref, pair_ref,
):
    observe(received_ref, matrix_ref, profile_ref, turned_ref, seen_ref)
    fill_pair(profile_ref, live_precision(count_ref, precision_ref) * seen_ref[...], pair_ref)
    spread_rows(matrix_ref, pair_ref, out_ref)


def observe_norm_kernel(
    count_ref, received_ref, precision_ref, profile_ref, matrix_ref, first_ref, second_ref,
    out_ref, turned_ref, seen_ref,
):
    observe(received_ref, matrix_ref, profile_ref, turned_ref, seen_ref)
    seen = seen_ref[...]
    lane = lax.broadcasted_iota(jnp.int32, out_ref.shape, 1)
    parts = (first_ref[0], second_ref[0], second_ref[1], live_precision(count_ref, precision_ref) * seen * seen)
    row = jnp.zeros(out_ref.shape, f32)
    for k in range(4):
        row = jnp.where(lane == k, jnp.sum(parts[k]), row)
    out_ref[...] = row


def split_pair(arrived_ref, pair_ref):
    slots, levels = arrived_ref.shape
    for base in range(0, slots, CHUNK):
        high, low = halves(arrived_ref[base : base + CHUNK, :])
        pair_ref[base : base + CHUNK, :levels] = high
        pair_ref[base : base + CHUNK, levels:] = low


def place_first_kernel(send_ref, arrived_ref, out_ref, matrix_ref, pair_ref):
    slots, levels = arrived_ref.shape
    split_pair(arrived_ref, pair_ref)
    size = 128
    shape = (size, CHUNK)
    column = lax.broadcasted_iota(jnp.int32, shape, 0).astype(f32).astype(bf16)
    one, zero = jnp.ones(shape, bf16), jnp.zeros(shape, bf16)
    for base in range(0, out_ref.shape[0], size):
        near = (send_ref[...] - base).astype(f32).astype(bf16)
        for at in range(0, slots, CHUNK):
            hit = jnp.broadcast_to(near[:, at : at + CHUNK], shape) == column
            matrix_ref[base : base + size, at : at + CHUNK] = jnp.where(hit, one, zero)
    both = mm(matrix_ref[...], pair_ref[...])
    out_ref[...] = both[:, :levels] + both[:, levels:]


def place_kernel(matrix_ref, arrived_ref, out_ref, pair_ref):
    levels = arrived_ref.shape[1]
    split_pair(arrived_ref, pair_ref)
    both = mm(matrix_ref[...], pair_ref[...])
    out_ref[...] = both[:, :levels] + both[:, levels:]


def spot(place_ref, sizes):
    return lax.div(place_ref[0], sizes[1]), lax.rem(place_ref[0], sizes[1])


def strip_kernel(sizes, place_ref, cells_ref, one_ref, two_ref, first_ref, second_ref):
    across, along, _ = cells_ref.shape
    odd = lax.rem(spot(place_ref, sizes)[1], 2)
    head_or_tail = pl.multiple_of((1 - odd) * (along - HALO), HALO)
    tail_or_head = pl.multiple_of(odd * (along - HALO), HALO)
    for target, at in ((first_ref, head_or_tail), (second_ref, tail_or_head)):
        for k, source in enumerate((one_ref, cells_ref, two_ref)):
            target[k * across : (k + 1) * across] = source[:, pl.ds(at, HALO), :]


def fill(at_x, at_y, target, cells_ref, one_ref, two_ref, first_ref, second_ref):
    across, along, _ = cells_ref.shape
    odd_x, odd_y = lax.rem(at_x, 2), lax.rem(at_y, 2)
    above = (1 - odd_x) * (across + HALO)
    below = odd_x * (across + HALO)
    target[HALO : HALO + across, HALO : HALO + along] = cells_ref[...]
    target[pl.ds(above, HALO), HALO : HALO + along] = one_ref[...]
    target[pl.ds(below, HALO), HALO : HALO + along] = two_ref[...]
    for source, at in ((first_ref, 1 - odd_y), (second_ref, odd_y)):
        start = pl.multiple_of(at * (along + HALO), HALO)
        for k, row in enumerate((above, HALO, below)):
            target[pl.ds(row, HALO), pl.ds(start, HALO), :] = source[k * across : (k + 1) * across]


def conduct_kernel(sizes, place_ref, cells_ref, one_ref, two_ref, first_ref, second_ref, east_ref, north_ref, field):
    wide, tall, levels = field.shape
    across, along, _ = cells_ref.shape
    at_x, at_y = spot(place_ref, sizes)
    fill(at_x, at_y, field, cells_ref, one_ref, two_ref, first_ref, second_ref)
    edges = (at_x == 0, at_x == sizes[0] - 1, at_y == 0, at_y == sizes[1] - 1)

    @pl.when(edges[0])
    def _():
        field[:HALO] = jnp.zeros((HALO, tall, levels), f32)

    @pl.when(edges[1])
    def _():
        field[HALO + across :] = jnp.zeros((HALO, tall, levels), f32)

    @pl.when(edges[2])
    def _():
        field[:, :HALO] = jnp.zeros((wide, HALO, levels), f32)

    @pl.when(edges[3])
    def _():
        field[:, HALO + along :] = jnp.zeros((wide, HALO, levels), f32)

    def one(i, carry):
        here = COUPLING * field[i]
        after = field[jnp.minimum(i + 1, wide - 1)]
        east_ref[i] = here * after
        north_ref[i, : tall - 1] = here[: tall - 1] * field[i, 1:]
        north_ref[i, tall - 1 :] = jnp.zeros((1, levels), f32)
        return carry

    lax.fori_loop(0, wide, one, 0)


def select_kernel(send_ref, out_ref):
    slots, columns = out_ref.shape
    size = 128
    lane = lax.broadcasted_iota(jnp.int32, (size, size), 1).astype(f32)

    def one(index, carry):
        base = pl.multiple_of(index * size, size)
        wanted = jnp.broadcast_to(send_ref[:, pl.ds(base, size)].astype(f32), (size, size)).T
        for at in range(0, columns, size):
            hit = jnp.where(wanted == lane + at, 1.0, 0.0)
            out_ref[pl.ds(base, size), at : at + size] = hit.astype(bf16)
        return carry

    lax.fori_loop(0, slots // size, one, 0)


def smooth_kernel(sizes, place_ref, select_ref, cells_ref, one_ref, two_ref, first_ref, second_ref, east, north, *rest):
    *given, half_ref, full_ref, out_ref, sums_ref, field = rest
    across, along, levels = cells_ref.shape
    wide, tall = across + 2 * HALO, along + 2 * HALO
    fill(*spot(place_ref, sizes), field, cells_ref, one_ref, two_ref, first_ref, second_ref)

    def sweep(k):
        def row(i, carry):
            here, inward = carry
            after = field[i + 1]
            outward = east[i] * (after - here)
            above = north[i] * (pltpu.roll(here, tall - 1, 0) - here)
            field[i] = here + ((outward - inward) + (above - pltpu.roll(above, 1, 0)))
            return after, outward

        here = field[k]
        lax.fori_loop(k, wide - k, row, (here, east[k - 1] * (here - field[k - 1])), unroll=4)

    def middle():
        return field[HALO : HALO + across, HALO : HALO + along]

    for k in range(1, PASSES + 1):
        sweep(k)
    half = middle()
    half_ref[...] = half
    if given:
        sums_ref[0] = jnp.sum((given[0][...] * half).reshape(-1, 8, levels), axis=0)
        sums_ref[1] = jnp.sum((half * half).reshape(-1, 8, levels), axis=0)
    else:
        sums_ref[0] = jnp.sum((half * half).reshape(-1, 8, levels), axis=0)
    for k in range(PASSES + 1, HALO + 1):
        sweep(k)
    full = middle()
    full_ref[...] = full
    columns = across * along
    pair = jnp.concatenate(halves(full.reshape(columns, levels)), axis=1)

    size = out_ref.shape[0] // 2
    for base in range(0, out_ref.shape[0], size):
        both = mm(select_ref[base : base + size, :], pair)
        out_ref[base : base + size, :] = both[:, :levels] + both[:, levels:]


def exact_sum(x, y):
    total = x + y
    part = total - x
    return total, (x - (total - part)) + (y - part)


def exact_product(x, y):
    def cut(value):
        scaled = 4097.0 * value
        high = scaled - (scaled - value)
        return high, value - high

    product = x * y
    (xh, xl), (yh, yl) = cut(x), cut(y)
    return product, ((xh * yh - product) + xh * yl + xl * yh) + xl * yl


def fraction(top, bottom):
    high = top[0] / bottom[0]
    product, rest = exact_product(high, bottom[0])
    return high, (((top[0] - product) - rest) + (top[1] - high * bottom[1])) / bottom[0]


def minus_product(x, y, z):
    product, rest = exact_product(y[0], z[0])
    return (x[0] - product) + ((x[1] - rest) - (y[0] * z[1] + y[1] * z[0]))


def finish_kernel(sums_ref, b_ref, sb_ref, p_ref, sp_ref, control_ref, increment_ref):
    total = sums_ref[...]
    error = jnp.zeros_like(total)
    while total.shape[0] > 1:
        half = total.shape[0] // 2
        total, more = exact_sum(total[:half], total[half:])
        error = (error[:half] + error[half:]) + more
    lane = lax.broadcasted_iota(jnp.int32, total.shape, 1)

    def pick(values, k):
        return jnp.sum(jnp.where(lane == k, values, 0.0), axis=1, keepdims=True)

    a, c, e, f = [(pick(total, k), pick(error, k)) for k in range(4)]
    slope, square, cube = fraction(c, a), fraction(e, a), fraction(f, a)
    first = 1.0 / (1.0 + slope[0])
    rest = minus_product(square, slope, slope)
    curved = rest + (minus_product(cube, slope, square) - slope[0] * rest)
    second = jnp.clip(rest / (curved - first * rest * rest), 0.0, 1.0)
    of_b = first + second * (first * first * rest + first * slope[0])
    of_p = -second * first
    control_ref[...] = of_b * b_ref[...] + of_p * p_ref[...]
    increment_ref[...] = of_b * sb_ref[...] + of_p * sp_ref[...]


def swap(cells, axis, odd):
    count = lax.axis_size(axis)
    pairs = [(i, (i + 1) % count) for i in range(odd, count, 2)]
    return lax.ppermute(cells, axis, pairs + [(j, i) for i, j in pairs])


def exchange(rows):
    return lax.all_to_all(rows, ("gx", "gy"), split_axis=0, concat_axis=0, tiled=True)


def params(mib):
    return pltpu.CompilerParams(vmem_limit_bytes=mib * MIB)


def cost(flops, size):
    return pl.CostEstimate(flops=flops, bytes_accessed=size, transcendentals=0)


def on_device(
    length_scale, innovation, observed_precision, profile_weight, stencil_weight, send_rows, stencil_rows, obs_count,
):
    across, along, levels = length_scale.shape
    owners, slot_count = send_rows.shape[1:]
    slots = owners * slot_count
    columns = across * along
    obs = innovation.shape[0]
    innovation = innovation.reshape(1, obs)
    precision = observed_precision.reshape(1, obs)
    sizes = tuple(lax.axis_size(axis) for axis in ("gx", "gy"))
    place = lax.axis_index(("gx", "gy")).astype(jnp.int32).reshape(1)

    whole = pl.BlockSpec(memory_space=pltpu.VMEM)
    scalar = pl.BlockSpec(memory_space=pltpu.SMEM)
    afar = pl.BlockSpec(memory_space=pltpu.HBM)
    slot_rows = jax.ShapeDtypeStruct((slots, levels), f32)
    tile = jax.ShapeDtypeStruct((across, along, levels), f32)
    strip = jax.ShapeDtypeStruct((across + 2 * HALO, HALO, levels), f32)
    grown = (across + 2 * HALO, along + 2 * HALO, levels)
    pair_scratch = pltpu.VMEM((2 * obs, 2 * levels), bf16)
    turned_scratch = pltpu.VMEM((2 * levels, slots), bf16)
    seen_scratch = pltpu.VMEM((1, obs), f32)

    def trade(rows):
        return exchange(rows.reshape(owners, slot_count, levels)).reshape(slots, levels)

    def strips(cells, one, two):
        return pl.pallas_call(
            functools.partial(strip_kernel, sizes),
            out_shape=(strip, strip),
            in_specs=[scalar] + [whole] * 3,
            out_specs=(whole, whole),
            compiler_params=params(2),
            name="strips",
        )(place, cells, one, two)

    def over_x(cells):
        return swap(cells, "gx", 0), swap(cells, "gx", 1)

    def over_y(first, second):
        return swap(first, "gy", 0), swap(second, "gy", 1)

    scale_x = over_x(length_scale)
    stencil_rows, place = lax.optimization_barrier((stencil_rows, place))
    turned = send_rows.transpose(0, 2, 1)
    given = (stencil_rows, stencil_weight, turned, innovation, precision, profile_weight)
    matrix, spread, send = pl.pallas_call(
        spread_first_kernel,
        out_shape=(
            jax.ShapeDtypeStruct((slots, 2 * obs), bf16),
            slot_rows,
            jax.ShapeDtypeStruct((1, slots), jnp.int32),
        ),
        in_specs=[scalar] + [afar] * 6,
        out_specs=(whole,) * 3,
        scratch_shapes=[
            *(pltpu.VMEM(x.shape, x.dtype) for x in given),
            pair_scratch,
            pltpu.SemaphoreType.DMA((6,)),
        ],
        compiler_params=params(14),
        cost_estimate=cost(8 << 30, 1 << 24),
        name="spread_first",
    )(obs_count, *(pltpu.with_memory_space_constraint(x, pltpu.HBM) for x in given))
    spread, *scale_x = lax.optimization_barrier((spread, *scale_x))
    arrived, send, *scale_x = lax.optimization_barrier((trade(spread), send, *scale_x))

    cells, placing = pl.pallas_call(
        place_first_kernel,
        out_shape=(jax.ShapeDtypeStruct((columns, levels), f32), jax.ShapeDtypeStruct((columns, slots), bf16)),
        in_specs=[whole, whole],
        out_specs=(whole, whole),
        scratch_shapes=[pltpu.VMEM((slots, 2 * levels), bf16)],
        compiler_params=params(8),
        name="place_first",
    )(send, arrived)
    selecting = pl.pallas_call(
        select_kernel,
        out_shape=jax.ShapeDtypeStruct((slots, columns), bf16),
        in_specs=[whole],
        out_specs=whole,
        compiler_params=params(2),
        cost_estimate=cost(1 << 28, 1 << 22),
        name="select",
    )(send)
    scale_y = over_y(*strips(length_scale, *scale_x))
    conductances = pl.pallas_call(
        functools.partial(conduct_kernel, sizes),
        out_shape=(jax.ShapeDtypeStruct(grown, f32),) * 2,
        in_specs=[scalar] + [whole] * 5,
        out_specs=(whole, whole),
        scratch_shapes=[pltpu.VMEM(grown, f32)],
        compiler_params=params(4),
        cost_estimate=cost(1 << 26, 1 << 22),
        name="conduct",
    )(place, length_scale, *scale_x, *scale_y)

    def smooth_twice(cells, given):
        cells = cells.reshape(across, along, levels)
        aside = over_x(cells)
        count = 1 + len(given)
        return pl.pallas_call(
            functools.partial(smooth_kernel, sizes),
            out_shape=(tile, tile, slot_rows, jax.ShapeDtypeStruct((count, 8, levels), f32)),
            in_specs=[scalar] + [whole] * (8 + len(given)),
            out_specs=(whole,) * 4,
            scratch_shapes=[pltpu.VMEM(grown, f32)],
            compiler_params=params(10),
            name="smooth",
        )(place, selecting, cells, *aside, *over_y(*strips(cells, *aside)), *conductances, *given)

    b, sb, outgoing, first_sums = smooth_twice(cells, ())

    spread = pl.pallas_call(
        observe_adjoint_kernel,
        out_shape=slot_rows,
        in_specs=[scalar] + [whole] * 4,
        out_specs=whole,
        scratch_shapes=[turned_scratch, seen_scratch, pair_scratch],
        compiler_params=params(16),
        name="observe_adjoint",
    )(obs_count, trade(outgoing), precision, profile_weight, matrix)

    cells = pl.pallas_call(
        place_kernel,
        out_shape=jax.ShapeDtypeStruct((columns, levels), f32),
        in_specs=[whole, whole],
        out_specs=whole,
        scratch_shapes=[pltpu.VMEM((slots, 2 * levels), bf16)],
        compiler_params=params(8),
        name="place",
    )(placing, trade(spread))
    p, sp, outgoing, second_sums = smooth_twice(cells, (b,))

    sums = pl.pallas_call(
        observe_norm_kernel,
        out_shape=jax.ShapeDtypeStruct((owners, levels), f32),
        in_specs=[scalar] + [whole] * 6,
        out_specs=whole,
        scratch_shapes=[turned_scratch, seen_scratch],
        compiler_params=params(14),
        name="observe_norm",
    )(obs_count, trade(outgoing), precision, profile_weight, matrix, first_sums, second_sums)

    sums = exchange(sums.reshape(owners, 1, levels)).reshape(owners, levels)

    return pl.pallas_call(
        finish_kernel,
        out_shape=(
            jax.ShapeDtypeStruct((columns, levels), f32),
            jax.ShapeDtypeStruct((columns, levels), f32),
        ),
        in_specs=[whole] * 5,
        out_specs=(whole, whole),
        compiler_params=params(4),
        name="finish",
    )(sums, *(x.reshape(columns, levels) for x in (b, sb, p, sp)))


def solution(mesh):
    def run(*args):
        control, increment = on_device(*args)
        shape = args[0].shape
        return control.reshape(shape), increment.reshape(shape)

    return jax.shard_map(
        run,
        mesh=mesh,
        in_specs=(
            P("gx", "gy", None),
            P(("gx", "gy")),
            P(("gx", "gy")),
            P(("gx", "gy"), None),
            P(None, ("gx", "gy")),
            P(("gx", "gy"), None, None),
            P(None, ("gx", "gy")),
            P(("gx", "gy")),
        ),
        out_specs=(P("gx", "gy", None), P("gx", "gy", None)),
        check_vma=False,
    )
```

```python
import functools

import jax
import jax.numpy as jnp
from jax import lax
from jax.experimental import pallas as pl
from jax.experimental.pallas import tpu as pltpu
from jax.sharding import PartitionSpec as P


MIB = 1 << 20
COUPLING = 0.12
PASSES = 4
HALO = 2 * PASSES
CHUNK = 256
bf16 = jnp.bfloat16
f32 = jnp.float32


def mm(lhs, rhs):
    return jnp.dot(lhs, rhs, preferred_element_type=f32)


def halves(values):
    high = values.astype(bf16)
    return high, (values - high.astype(f32)).astype(bf16)


def live_precision(count_ref, precision_ref):
    place = lax.broadcasted_iota(jnp.int32, precision_ref.shape, 1)
    return jnp.where(place < count_ref[0], precision_ref[...], 0.0)


def merge_repeats(rows_ref, weights_ref):
    rows = [rows_ref[k : k + 1, :] for k in range(4)]
    weights = [weights_ref[k : k + 1, :] for k in range(4)]
    for k in range(1, 4):
        for j in range(k):
            same = rows[k] == rows[j]
            weights[j] = weights[j] + jnp.where(same, weights[k], 0.0)
            weights[k] = jnp.where(same, 0.0, weights[k])
    return rows, [halves(weight) for weight in weights]


def flatten_send(send_ref, out_ref):
    _, slot_count, owners = send_ref.shape
    lanes = 128
    group = lanes // slot_count
    wide = lax.broadcasted_iota(jnp.int32, (slot_count, lanes), 1)
    tall = lax.broadcasted_iota(jnp.int32, (slot_count, lanes), 0)
    again = jnp.where(lax.rem(wide, slot_count) == tall, 1.0, 0.0)
    repeated = jnp.dot(
        send_ref[0].astype(f32).T, again, precision=lax.Precision.HIGHEST, preferred_element_type=f32
    )
    owner = lax.broadcasted_iota(jnp.int32, (owners, lanes), 0)
    lane = lax.broadcasted_iota(jnp.int32, (owners, lanes), 1)
    kept = jnp.where(lax.div(lane, slot_count) == lax.rem(owner, group), repeated, 0.0)
    lines = jnp.sum(kept.reshape(owners // group, group, lanes), axis=1).astype(jnp.int32)
    for k in range(owners // group):
        out_ref[:, k * lanes : (k + 1) * lanes] = lines[k : k + 1]


def spread_first_kernel(
    count_ref, rows_hbm, weights_hbm, send_hbm, innovation_hbm, precision_hbm, profile_hbm,
    matrix_ref, out_ref, flat_ref,
    rows_ref, weights_ref, send_ref, innovation_ref, precision_ref, profile_ref, pair_ref, sems,
):
    moves = (
        (rows_hbm, rows_ref), (weights_hbm, weights_ref), (send_hbm, send_ref),
        (innovation_hbm, innovation_ref), (precision_hbm, precision_ref), (profile_hbm, profile_ref),
    )
    copies = [pltpu.make_async_copy(*move, sems.at[k]) for k, move in enumerate(moves)]
    for copy in copies:
        copy.start()
    for copy in copies[:5]:
        copy.wait()
    flatten_send(send_ref, flat_ref)
    rows, parts = merge_repeats(rows_ref, weights_ref)
    forcing = live_precision(count_ref, precision_ref) * innovation_ref[...]
    copies[5].wait()
    fill_pair(profile_ref, forcing, pair_ref)
    slots, obs, levels = matrix_ref.shape[0], rows_ref.shape[1], out_ref.shape[1]
    shape = (CHUNK, CHUNK)
    slot = lax.broadcasted_iota(jnp.int32, shape, 0).astype(f32).astype(bf16)

    def one(index, carry):
        base = pl.multiple_of(index * CHUNK, CHUNK)
        near = [(row - base).astype(f32).astype(bf16) for row in rows]
        for at in range(0, obs, CHUNK):
            high = jnp.zeros(shape, bf16)
            low = jnp.zeros(shape, bf16)
            for k in (3, 2, 1, 0):
                cut = slice(at, at + CHUNK)
                hit = jnp.broadcast_to(near[k][:, cut], shape) == slot
                high = jnp.where(hit, jnp.broadcast_to(parts[k][0][:, cut], shape), high)
                low = jnp.where(hit, jnp.broadcast_to(parts[k][1][:, cut], shape), low)
            matrix_ref[pl.ds(base, CHUNK), at : at + CHUNK] = high
            matrix_ref[pl.ds(base, CHUNK), obs + at : obs + at + CHUNK] = low
        both = mm(matrix_ref[pl.ds(base, CHUNK), :], pair_ref[...])
        out_ref[pl.ds(base, CHUNK), :] = both[:, :levels] + both[:, levels:]
        return carry

    lax.fori_loop(0, slots // CHUNK, one, 0)


def spread_rows(matrix_ref, pair_ref, out_ref):
    slots, levels = out_ref.shape
    size = slots // 2
    for base in range(0, slots, size):
        both = mm(matrix_ref[base : base + size, :], pair_ref[...])
        out_ref[base : base + size, :] = both[:, :levels] + both[:, levels:]


def fill_pair(profile_ref, forcing, pair_ref):
    obs, levels = profile_ref.shape
    for at in range(0, obs, levels):
        column = jnp.broadcast_to(forcing[:, at : at + levels], (levels, levels)).T
        high, low = halves(profile_ref[at : at + levels, :] * column)
        for base in (at, obs + at):
            pair_ref[base : base + levels, :levels] = high
            pair_ref[base : base + levels, levels:] = low


def observe(received_ref, matrix_ref, profile_ref, turned_ref, seen_ref):
    slots, levels = received_ref.shape
    obs = profile_ref.shape[0]
    for at in range(0, slots, levels):
        high, low = halves(received_ref[at : at + levels, :].T)
        turned_ref[:levels, at : at + levels] = high
        turned_ref[levels:, at : at + levels] = low
    size = obs // 2
    for base in range(0, obs, size):
        both = mm(turned_ref[...], matrix_ref[:, base : base + size])
        gathered = both[:levels] + both[levels:]
        gathered = gathered + mm(turned_ref[:levels], matrix_ref[:, obs + base : obs + base + size])
        seen_ref[:, base : base + size] = jnp.sum(
            profile_ref[base : base + size, :].T * gathered, axis=0, keepdims=True
        )


def observe_adjoint_kernel(
    count_ref, received_ref, precision_ref, profile_ref, matrix_ref, out_ref, turned_ref, seen_ref, pair_ref,
):
    observe(received_ref, matrix_ref, profile_ref, turned_ref, seen_ref)
    fill_pair(profile_ref, live_precision(count_ref, precision_ref) * seen_ref[...], pair_ref)
    spread_rows(matrix_ref, pair_ref, out_ref)


def observe_norm_kernel(
    count_ref, received_ref, precision_ref, profile_ref, matrix_ref, first_ref, second_ref,
    out_ref, turned_ref, seen_ref,
):
    slots, levels = received_ref.shape
    obs = profile_ref.shape[0]
    for at in range(0, slots, levels):
        turned_ref[:, at : at + levels] = received_ref[at : at + levels, :].T.astype(bf16)
    size = obs // 2
    for base in range(0, obs, size):
        gathered = mm(turned_ref[...], matrix_ref[:, base : base + size]) + mm(
            turned_ref[...], matrix_ref[:, obs + base : obs + base + size]
        )
        seen_ref[:, base : base + size] = jnp.sum(
            profile_ref[base : base + size, :].T * gathered, axis=0, keepdims=True
        )
    seen = seen_ref[...]
    lane = lax.broadcasted_iota(jnp.int32, out_ref.shape, 1)
    parts = (first_ref[0], second_ref[0], second_ref[1], live_precision(count_ref, precision_ref) * seen * seen)
    row = jnp.zeros(out_ref.shape, f32)
    for k in range(4):
        row = jnp.where(lane == k, jnp.sum(parts[k]), row)
    out_ref[...] = row


def split_pair(arrived_ref, pair_ref):
    slots, levels = arrived_ref.shape
    for base in range(0, slots, CHUNK):
        high, low = halves(arrived_ref[base : base + CHUNK, :])
        pair_ref[base : base + CHUNK, :levels] = high
        pair_ref[base : base + CHUNK, levels:] = low


def place_first_kernel(send_ref, arrived_ref, out_ref, matrix_ref, pair_ref):
    slots, levels = arrived_ref.shape
    split_pair(arrived_ref, pair_ref)
    size = 128
    shape = (size, CHUNK)
    column = lax.broadcasted_iota(jnp.int32, shape, 0).astype(f32).astype(bf16)
    one, zero = jnp.ones(shape, bf16), jnp.zeros(shape, bf16)
    for base in range(0, out_ref.shape[0], size):
        near = (send_ref[...] - base).astype(f32).astype(bf16)
        for at in range(0, slots, CHUNK):
            hit = jnp.broadcast_to(near[:, at : at + CHUNK], shape) == column
            matrix_ref[base : base + size, at : at + CHUNK] = jnp.where(hit, one, zero)
    both = mm(matrix_ref[...], pair_ref[...])
    out_ref[...] = both[:, :levels] + both[:, levels:]


def place_kernel(matrix_ref, arrived_ref, out_ref, pair_ref):
    levels = arrived_ref.shape[1]
    split_pair(arrived_ref, pair_ref)
    both = mm(matrix_ref[...], pair_ref[...])
    out_ref[...] = both[:, :levels] + both[:, levels:]


def spot(place_ref, sizes):
    return lax.div(place_ref[0], sizes[1]), lax.rem(place_ref[0], sizes[1])


def strip_kernel(sizes, place_ref, cells_ref, one_ref, two_ref, first_ref, second_ref):
    across, along, _ = cells_ref.shape
    odd = lax.rem(spot(place_ref, sizes)[1], 2)
    head_or_tail = pl.multiple_of((1 - odd) * (along - HALO), HALO)
    tail_or_head = pl.multiple_of(odd * (along - HALO), HALO)
    for target, at in ((first_ref, head_or_tail), (second_ref, tail_or_head)):
        for k, source in enumerate((one_ref, cells_ref, two_ref)):
            target[k * across : (k + 1) * across] = source[:, pl.ds(at, HALO), :]


def fill(at_x, at_y, target, cells_ref, one_ref, two_ref, first_ref, second_ref):
    across, along, _ = cells_ref.shape
    odd_x, odd_y = lax.rem(at_x, 2), lax.rem(at_y, 2)
    above = (1 - odd_x) * (across + HALO)
    below = odd_x * (across + HALO)
    target[HALO : HALO + across, HALO : HALO + along] = cells_ref[...]
    target[pl.ds(above, HALO), HALO : HALO + along] = one_ref[...]
    target[pl.ds(below, HALO), HALO : HALO + along] = two_ref[...]
    for source, at in ((first_ref, 1 - odd_y), (second_ref, odd_y)):
        start = pl.multiple_of(at * (along + HALO), HALO)
        for k, row in enumerate((above, HALO, below)):
            target[pl.ds(row, HALO), pl.ds(start, HALO), :] = source[k * across : (k + 1) * across]


def conduct_kernel(sizes, place_ref, cells_ref, one_ref, two_ref, first_ref, second_ref, east_ref, north_ref, field):
    wide, tall, levels = field.shape
    across, along, _ = cells_ref.shape
    at_x, at_y = spot(place_ref, sizes)
    fill(at_x, at_y, field, cells_ref, one_ref, two_ref, first_ref, second_ref)
    edges = (at_x == 0, at_x == sizes[0] - 1, at_y == 0, at_y == sizes[1] - 1)

    @pl.when(edges[0])
    def _():
        field[:HALO] = jnp.zeros((HALO, tall, levels), f32)

    @pl.when(edges[1])
    def _():
        field[HALO + across :] = jnp.zeros((HALO, tall, levels), f32)

    @pl.when(edges[2])
    def _():
        field[:, :HALO] = jnp.zeros((wide, HALO, levels), f32)

    @pl.when(edges[3])
    def _():
        field[:, HALO + along :] = jnp.zeros((wide, HALO, levels), f32)

    def one(i, carry):
        here = COUPLING * field[i]
        after = field[jnp.minimum(i + 1, wide - 1)]
        east_ref[i] = here * after
        north_ref[i, : tall - 1] = here[: tall - 1] * field[i, 1:]
        north_ref[i, tall - 1 :] = jnp.zeros((1, levels), f32)
        return carry

    lax.fori_loop(0, wide, one, 0)


def select_kernel(send_ref, out_ref):
    slots, columns = out_ref.shape
    size = 128
    lane = lax.broadcasted_iota(jnp.int32, (size, size), 1).astype(f32)

    def one(index, carry):
        base = pl.multiple_of(index * size, size)
        wanted = jnp.broadcast_to(send_ref[:, pl.ds(base, size)].astype(f32), (size, size)).T
        for at in range(0, columns, size):
            hit = jnp.where(wanted == lane + at, 1.0, 0.0)
            out_ref[pl.ds(base, size), at : at + size] = hit.astype(bf16)
        return carry

    lax.fori_loop(0, slots // size, one, 0)


def smooth_kernel(sizes, place_ref, select_ref, cells_ref, one_ref, two_ref, first_ref, second_ref, east, north, *rest):
    *given, half_ref, full_ref, out_ref, sums_ref, field = rest
    across, along, levels = cells_ref.shape
    wide, tall = across + 2 * HALO, along + 2 * HALO
    fill(*spot(place_ref, sizes), field, cells_ref, one_ref, two_ref, first_ref, second_ref)

    def sweep(k):
        def row(i, carry):
            here, inward = carry
            after = field[i + 1]
            outward = east[i] * (after - here)
            above = north[i] * (pltpu.roll(here, tall - 1, 0) - here)
            field[i] = here + ((outward - inward) + (above - pltpu.roll(above, 1, 0)))
            return after, outward

        here = field[k]
        lax.fori_loop(k, wide - k, row, (here, east[k - 1] * (here - field[k - 1])), unroll=4)

    def middle():
        return field[HALO : HALO + across, HALO : HALO + along]

    for k in range(1, PASSES + 1):
        sweep(k)
    half = middle()
    half_ref[...] = half
    if given:
        sums_ref[0] = jnp.sum((given[0][...] * half).reshape(-1, 8, levels), axis=0)
        sums_ref[1] = jnp.sum((half * half).reshape(-1, 8, levels), axis=0)
    else:
        sums_ref[0] = jnp.sum((half * half).reshape(-1, 8, levels), axis=0)
    for k in range(PASSES + 1, HALO + 1):
        sweep(k)
    full = middle()
    full_ref[...] = full
    columns = across * along
    pair = jnp.concatenate(halves(full.reshape(columns, levels)), axis=1)

    size = out_ref.shape[0] // 2
    for base in range(0, out_ref.shape[0], size):
        both = mm(select_ref[base : base + size, :], pair)
        out_ref[base : base + size, :] = both[:, :levels] + both[:, levels:]


def exact_sum(x, y):
    total = x + y
    part = total - x
    return total, (x - (total - part)) + (y - part)


def exact_product(x, y):
    def cut(value):
        scaled = 4097.0 * value
        high = scaled - (scaled - value)
        return high, value - high

    product = x * y
    (xh, xl), (yh, yl) = cut(x), cut(y)
    return product, ((xh * yh - product) + xh * yl + xl * yh) + xl * yl


def fraction(top, bottom):
    high = top[0] / bottom[0]
    product, rest = exact_product(high, bottom[0])
    return high, (((top[0] - product) - rest) + (top[1] - high * bottom[1])) / bottom[0]


def minus_product(x, y, z):
    product, rest = exact_product(y[0], z[0])
    return (x[0] - product) + ((x[1] - rest) - (y[0] * z[1] + y[1] * z[0]))


def finish_kernel(sums_ref, b_ref, sb_ref, p_ref, sp_ref, control_ref, increment_ref):
    total = sums_ref[...]
    error = jnp.zeros_like(total)
    while total.shape[0] > 1:
        half = total.shape[0] // 2
        total, more = exact_sum(total[:half], total[half:])
        error = (error[:half] + error[half:]) + more
    lane = lax.broadcasted_iota(jnp.int32, total.shape, 1)

    def pick(values, k):
        return jnp.sum(jnp.where(lane == k, values, 0.0), axis=1, keepdims=True)

    a, c, e, f = [(pick(total, k), pick(error, k)) for k in range(4)]
    slope, square, cube = fraction(c, a), fraction(e, a), fraction(f, a)
    first = 1.0 / (1.0 + slope[0])
    rest = minus_product(square, slope, slope)
    curved = rest + (minus_product(cube, slope, square) - slope[0] * rest)
    second = jnp.clip(rest / (curved - first * rest * rest), 0.0, 1.0)
    of_b = first + second * (first * first * rest + first * slope[0])
    of_p = -second * first
    control_ref[...] = of_b * b_ref[...] + of_p * p_ref[...]
    increment_ref[...] = of_b * sb_ref[...] + of_p * sp_ref[...]


def swap(cells, axis, odd):
    count = lax.axis_size(axis)
    pairs = [(i, (i + 1) % count) for i in range(odd, count, 2)]
    return lax.ppermute(cells, axis, pairs + [(j, i) for i, j in pairs])


def exchange(rows):
    return lax.all_to_all(rows, ("gx", "gy"), split_axis=0, concat_axis=0, tiled=True)


def params(mib):
    return pltpu.CompilerParams(vmem_limit_bytes=mib * MIB)


def cost(flops, size):
    return pl.CostEstimate(flops=flops, bytes_accessed=size, transcendentals=0)


def on_device(
    length_scale, innovation, observed_precision, profile_weight, stencil_weight, send_rows, stencil_rows, obs_count,
):
    across, along, levels = length_scale.shape
    owners, slot_count = send_rows.shape[1:]
    slots = owners * slot_count
    columns = across * along
    obs = innovation.shape[0]
    innovation = innovation.reshape(1, obs)
    precision = observed_precision.reshape(1, obs)
    sizes = tuple(lax.axis_size(axis) for axis in ("gx", "gy"))
    place = lax.axis_index(("gx", "gy")).astype(jnp.int32).reshape(1)

    whole = pl.BlockSpec(memory_space=pltpu.VMEM)
    scalar = pl.BlockSpec(memory_space=pltpu.SMEM)
    afar = pl.BlockSpec(memory_space=pltpu.HBM)
    slot_rows = jax.ShapeDtypeStruct((slots, levels), f32)
    tile = jax.ShapeDtypeStruct((across, along, levels), f32)
    strip = jax.ShapeDtypeStruct((across + 2 * HALO, HALO, levels), f32)
    grown = (across + 2 * HALO, along + 2 * HALO, levels)
    pair_scratch = pltpu.VMEM((2 * obs, 2 * levels), bf16)
    turned_scratch = pltpu.VMEM((2 * levels, slots), bf16)
    seen_scratch = pltpu.VMEM((1, obs), f32)

    def trade(rows):
        return exchange(rows.reshape(owners, slot_count, levels)).reshape(slots, levels)

    def strips(cells, one, two):
        return pl.pallas_call(
            functools.partial(strip_kernel, sizes),
            out_shape=(strip, strip),
            in_specs=[scalar] + [whole] * 3,
            out_specs=(whole, whole),
            compiler_params=params(2),
            name="strips",
        )(place, cells, one, two)

    def over_x(cells):
        return swap(cells, "gx", 0), swap(cells, "gx", 1)

    def over_y(first, second):
        return swap(first, "gy", 0), swap(second, "gy", 1)

    scale_x = over_x(length_scale)
    stencil_rows, place = lax.optimization_barrier((stencil_rows, place))
    turned = send_rows.transpose(0, 2, 1)
    given = (stencil_rows, stencil_weight, turned, innovation, precision, profile_weight)
    matrix, spread, send = pl.pallas_call(
        spread_first_kernel,
        out_shape=(
            jax.ShapeDtypeStruct((slots, 2 * obs), bf16),
            slot_rows,
            jax.ShapeDtypeStruct((1, slots), jnp.int32),
        ),
        in_specs=[scalar] + [afar] * 6,
        out_specs=(whole,) * 3,
        scratch_shapes=[
            *(pltpu.VMEM(x.shape, x.dtype) for x in given),
            pair_scratch,
            pltpu.SemaphoreType.DMA((6,)),
        ],
        compiler_params=params(14),
        cost_estimate=cost(8 << 30, 1 << 24),
        name="spread_first",
    )(obs_count, *(pltpu.with_memory_space_constraint(x, pltpu.HBM) for x in given))
    spread, *scale_x = lax.optimization_barrier((spread, *scale_x))
    arrived, send, *scale_x = lax.optimization_barrier((trade(spread), send, *scale_x))

    cells, placing = pl.pallas_call(
        place_first_kernel,
        out_shape=(jax.ShapeDtypeStruct((columns, levels), f32), jax.ShapeDtypeStruct((columns, slots), bf16)),
        in_specs=[whole, whole],
        out_specs=(whole, whole),
        scratch_shapes=[pltpu.VMEM((slots, 2 * levels), bf16)],
        compiler_params=params(8),
        name="place_first",
    )(send, arrived)
    selecting = pl.pallas_call(
        select_kernel,
        out_shape=jax.ShapeDtypeStruct((slots, columns), bf16),
        in_specs=[whole],
        out_specs=whole,
        compiler_params=params(2),
        cost_estimate=cost(1 << 28, 1 << 22),
        name="select",
    )(send)
    scale_y = over_y(*strips(length_scale, *scale_x))
    conductances = pl.pallas_call(
        functools.partial(conduct_kernel, sizes),
        out_shape=(jax.ShapeDtypeStruct(grown, f32),) * 2,
        in_specs=[scalar] + [whole] * 5,
        out_specs=(whole, whole),
        scratch_shapes=[pltpu.VMEM(grown, f32)],
        compiler_params=params(4),
        cost_estimate=cost(1 << 26, 1 << 22),
        name="conduct",
    )(place, length_scale, *scale_x, *scale_y)

    def smooth_twice(cells, given):
        cells = cells.reshape(across, along, levels)
        aside = over_x(cells)
        count = 1 + len(given)
        return pl.pallas_call(
            functools.partial(smooth_kernel, sizes),
            out_shape=(tile, tile, slot_rows, jax.ShapeDtypeStruct((count, 8, levels), f32)),
            in_specs=[scalar] + [whole] * (8 + len(given)),
            out_specs=(whole,) * 4,
            scratch_shapes=[pltpu.VMEM(grown, f32)],
            compiler_params=params(10),
            name="smooth",
        )(place, selecting, cells, *aside, *over_y(*strips(cells, *aside)), *conductances, *given)

    b, sb, outgoing, first_sums = smooth_twice(cells, ())

    spread = pl.pallas_call(
        observe_adjoint_kernel,
        out_shape=slot_rows,
        in_specs=[scalar] + [whole] * 4,
        out_specs=whole,
        scratch_shapes=[turned_scratch, seen_scratch, pair_scratch],
        compiler_params=params(16),
        name="observe_adjoint",
    )(obs_count, trade(outgoing), precision, profile_weight, matrix)

    cells = pl.pallas_call(
        place_kernel,
        out_shape=jax.ShapeDtypeStruct((columns, levels), f32),
        in_specs=[whole, whole],
        out_specs=whole,
        scratch_shapes=[pltpu.VMEM((slots, 2 * levels), bf16)],
        compiler_params=params(8),
        name="place",
    )(placing, trade(spread))
    p, sp, outgoing, second_sums = smooth_twice(cells, (b,))

    sums = pl.pallas_call(
        observe_norm_kernel,
        out_shape=jax.ShapeDtypeStruct((owners, levels), f32),
        in_specs=[scalar] + [whole] * 6,
        out_specs=whole,
        scratch_shapes=[pltpu.VMEM((levels, slots), bf16), seen_scratch],
        compiler_params=params(14),
        name="observe_norm",
    )(obs_count, trade(outgoing), precision, profile_weight, matrix, first_sums, second_sums)

    sums = exchange(sums.reshape(owners, 1, levels)).reshape(owners, levels)

    return pl.pallas_call(
        finish_kernel,
        out_shape=(
            jax.ShapeDtypeStruct((columns, levels), f32),
            jax.ShapeDtypeStruct((columns, levels), f32),
        ),
        in_specs=[whole] * 5,
        out_specs=(whole, whole),
        compiler_params=params(4),
        name="finish",
    )(sums, *(x.reshape(columns, levels) for x in (b, sb, p, sp)))


def solution(mesh):
    def run(*args):
        control, increment = on_device(*args)
        shape = args[0].shape
        return control.reshape(shape), increment.reshape(shape)

    return jax.shard_map(
        run,
        mesh=mesh,
        in_specs=(
            P("gx", "gy", None),
            P(("gx", "gy")),
            P(("gx", "gy")),
            P(("gx", "gy"), None),
            P(None, ("gx", "gy")),
            P(("gx", "gy"), None, None),
            P(None, ("gx", "gy")),
            P(("gx", "gy")),
        ),
        out_specs=(P("gx", "gy", None), P("gx", "gy", None)),
        check_vma=False,
    )
```

```python
import functools

import jax
import jax.numpy as jnp
from jax import lax
from jax.experimental import pallas as pl
from jax.experimental.pallas import tpu as pltpu
from jax.sharding import PartitionSpec as P


MIB = 1 << 20
COUPLING = 0.12
PASSES = 4
HALO = 2 * PASSES
CHUNK = 256
bf16 = jnp.bfloat16
f32 = jnp.float32


def mm(lhs, rhs):
    return jnp.dot(lhs, rhs, preferred_element_type=f32)


def halves(values):
    high = values.astype(bf16)
    return high, (values - high.astype(f32)).astype(bf16)


def live_precision(count_ref, precision_ref):
    place = lax.broadcasted_iota(jnp.int32, precision_ref.shape, 1)
    return jnp.where(place < count_ref[0], precision_ref[...], 0.0)


def merge_repeats(rows_ref, weights_ref):
    rows = [rows_ref[k : k + 1, :] for k in range(4)]
    weights = [weights_ref[k : k + 1, :] for k in range(4)]
    for k in range(1, 4):
        for j in range(k):
            same = rows[k] == rows[j]
            weights[j] = weights[j] + jnp.where(same, weights[k], 0.0)
            weights[k] = jnp.where(same, 0.0, weights[k])
    return rows, [halves(weight) for weight in weights]


def flatten_send(send_ref, out_ref):
    _, slot_count, owners = send_ref.shape
    lanes = 128
    group = lanes // slot_count
    wide = lax.broadcasted_iota(jnp.int32, (slot_count, lanes), 1)
    tall = lax.broadcasted_iota(jnp.int32, (slot_count, lanes), 0)
    again = jnp.where(lax.rem(wide, slot_count) == tall, 1.0, 0.0)
    repeated = jnp.dot(
        send_ref[0].astype(f32).T, again, precision=lax.Precision.HIGHEST, preferred_element_type=f32
    )
    owner = lax.broadcasted_iota(jnp.int32, (owners, lanes), 0)
    lane = lax.broadcasted_iota(jnp.int32, (owners, lanes), 1)
    kept = jnp.where(lax.div(lane, slot_count) == lax.rem(owner, group), repeated, 0.0)
    lines = jnp.sum(kept.reshape(owners // group, group, lanes), axis=1).astype(jnp.int32)
    for k in range(owners // group):
        out_ref[:, k * lanes : (k + 1) * lanes] = lines[k : k + 1]


def spread_first_kernel(
    count_ref, rows_hbm, weights_hbm, send_hbm, innovation_hbm, precision_hbm, profile_hbm,
    matrix_ref, out_ref, flat_ref,
    rows_ref, weights_ref, send_ref, innovation_ref, precision_ref, profile_ref, pair_ref, sems,
):
    moves = (
        (rows_hbm, rows_ref), (weights_hbm, weights_ref), (send_hbm, send_ref),
        (innovation_hbm, innovation_ref), (precision_hbm, precision_ref), (profile_hbm, profile_ref),
    )
    copies = [pltpu.make_async_copy(*move, sems.at[k]) for k, move in enumerate(moves)]
    for copy in copies:
        copy.start()
    for copy in copies[:5]:
        copy.wait()
    flatten_send(send_ref, flat_ref)
    rows, parts = merge_repeats(rows_ref, weights_ref)
    forcing = live_precision(count_ref, precision_ref) * innovation_ref[...]
    copies[5].wait()
    fill_pair(profile_ref, forcing, pair_ref)
    slots, obs, levels = matrix_ref.shape[0], rows_ref.shape[1], out_ref.shape[1]
    shape = (CHUNK, CHUNK)
    slot = lax.broadcasted_iota(jnp.int32, shape, 0).astype(f32).astype(bf16)

    def one(index, carry):
        base = pl.multiple_of(index * CHUNK, CHUNK)
        near = [(row - base).astype(f32).astype(bf16) for row in rows]
        for at in range(0, obs, CHUNK):
            high = jnp.zeros(shape, bf16)
            low = jnp.zeros(shape, bf16)
            for k in (3, 2, 1, 0):
                cut = slice(at, at + CHUNK)
                hit = jnp.broadcast_to(near[k][:, cut], shape) == slot
                high = jnp.where(hit, jnp.broadcast_to(parts[k][0][:, cut], shape), high)
                low = jnp.where(hit, jnp.broadcast_to(parts[k][1][:, cut], shape), low)
            matrix_ref[pl.ds(base, CHUNK), at : at + CHUNK] = high
            matrix_ref[pl.ds(base, CHUNK), obs + at : obs + at + CHUNK] = low
        both = mm(matrix_ref[pl.ds(base, CHUNK), :], pair_ref[...])
        out_ref[pl.ds(base, CHUNK), :] = both[:, :levels] + both[:, levels:]
        return carry

    lax.fori_loop(0, slots // CHUNK, one, 0)


def spread_rows(matrix_ref, pair_ref, out_ref):
    slots, levels = out_ref.shape
    size = slots // 2
    for base in range(0, slots, size):
        both = mm(matrix_ref[base : base + size, :], pair_ref[...])
        out_ref[base : base + size, :] = both[:, :levels] + both[:, levels:]


def fill_pair(profile_ref, forcing, pair_ref):
    obs, levels = profile_ref.shape
    for at in range(0, obs, levels):
        column = jnp.broadcast_to(forcing[:, at : at + levels], (levels, levels)).T
        high, low = halves(profile_ref[at : at + levels, :] * column)
        for base in (at, obs + at):
            pair_ref[base : base + levels, :levels] = high
            pair_ref[base : base + levels, levels:] = low


def observe(received_ref, matrix_ref, profile_ref, upright_ref, turned_ref, seen_ref):
    slots, levels = received_ref.shape
    obs = profile_ref.shape[0]
    for at in range(0, slots, levels):
        high, low = halves(received_ref[at : at + levels, :].T)
        turned_ref[:levels, at : at + levels] = high
        turned_ref[levels:, at : at + levels] = low
    size = obs // 2
    for base in range(0, obs, size):
        both = mm(turned_ref[...], matrix_ref[:, base : base + size])
        gathered = both[:levels] + both[levels:]
        gathered = gathered + mm(turned_ref[:levels], matrix_ref[:, obs + base : obs + base + size])
        upright = profile_ref[base : base + size, :].T
        upright_ref[:, base : base + size] = upright
        seen_ref[:, base : base + size] = jnp.sum(upright * gathered, axis=0, keepdims=True)


def observe_adjoint_kernel(
    count_ref, received_ref, precision_ref, profile_ref, matrix_ref, out_ref, upright_ref, turned_ref, seen_ref, pair_ref,
):
    observe(received_ref, matrix_ref, profile_ref, upright_ref, turned_ref, seen_ref)
    fill_pair(profile_ref, live_precision(count_ref, precision_ref) * seen_ref[...], pair_ref)
    spread_rows(matrix_ref, pair_ref, out_ref)


def observe_norm_kernel(
    count_ref, received_ref, precision_ref, upright_ref, matrix_ref, first_ref, second_ref,
    out_ref, turned_ref, seen_ref,
):
    slots, levels = received_ref.shape
    obs = upright_ref.shape[1]
    for at in range(0, slots, levels):
        turned_ref[:, at : at + levels] = received_ref[at : at + levels, :].T.astype(bf16)
    size = obs // 2
    for base in range(0, obs, size):
        gathered = mm(turned_ref[...], matrix_ref[:, base : base + size]) + mm(
            turned_ref[...], matrix_ref[:, obs + base : obs + base + size]
        )
        seen_ref[:, base : base + size] = jnp.sum(
            upright_ref[:, base : base + size] * gathered, axis=0, keepdims=True
        )
    seen = seen_ref[...]
    lane = lax.broadcasted_iota(jnp.int32, out_ref.shape, 1)
    parts = (first_ref[0], second_ref[0], second_ref[1], live_precision(count_ref, precision_ref) * seen * seen)
    row = jnp.zeros(out_ref.shape, f32)
    for k in range(4):
        row = jnp.where(lane == k, jnp.sum(parts[k]), row)
    out_ref[...] = row


def split_pair(arrived_ref, pair_ref):
    slots, levels = arrived_ref.shape
    for base in range(0, slots, CHUNK):
        high, low = halves(arrived_ref[base : base + CHUNK, :])
        pair_ref[base : base + CHUNK, :levels] = high
        pair_ref[base : base + CHUNK, levels:] = low


def place_first_kernel(send_ref, arrived_ref, out_ref, matrix_ref, pair_ref):
    slots, levels = arrived_ref.shape
    split_pair(arrived_ref, pair_ref)
    size = 128
    shape = (size, CHUNK)
    column = lax.broadcasted_iota(jnp.int32, shape, 0).astype(f32).astype(bf16)
    one, zero = jnp.ones(shape, bf16), jnp.zeros(shape, bf16)
    for base in range(0, out_ref.shape[0], size):
        near = (send_ref[...] - base).astype(f32).astype(bf16)
        for at in range(0, slots, CHUNK):
            hit = jnp.broadcast_to(near[:, at : at + CHUNK], shape) == column
            matrix_ref[base : base + size, at : at + CHUNK] = jnp.where(hit, one, zero)
    both = mm(matrix_ref[...], pair_ref[...])
    out_ref[...] = both[:, :levels] + both[:, levels:]


def place_kernel(matrix_ref, arrived_ref, out_ref, pair_ref):
    levels = arrived_ref.shape[1]
    split_pair(arrived_ref, pair_ref)
    both = mm(matrix_ref[...], pair_ref[...])
    out_ref[...] = both[:, :levels] + both[:, levels:]


def spot(place_ref, sizes):
    return lax.div(place_ref[0], sizes[1]), lax.rem(place_ref[0], sizes[1])


def strip_kernel(sizes, place_ref, cells_ref, one_ref, two_ref, first_ref, second_ref):
    across, along, _ = cells_ref.shape
    odd = lax.rem(spot(place_ref, sizes)[1], 2)
    head_or_tail = pl.multiple_of((1 - odd) * (along - HALO), HALO)
    tail_or_head = pl.multiple_of(odd * (along - HALO), HALO)
    for target, at in ((first_ref, head_or_tail), (second_ref, tail_or_head)):
        for k, source in enumerate((one_ref, cells_ref, two_ref)):
            target[k * across : (k + 1) * across] = source[:, pl.ds(at, HALO), :]


def fill(at_x, at_y, target, cells_ref, one_ref, two_ref, first_ref, second_ref):
    across, along, _ = cells_ref.shape
    odd_x, odd_y = lax.rem(at_x, 2), lax.rem(at_y, 2)
    above = (1 - odd_x) * (across + HALO)
    below = odd_x * (across + HALO)
    target[HALO : HALO + across, HALO : HALO + along] = cells_ref[...]
    target[pl.ds(above, HALO), HALO : HALO + along] = one_ref[...]
    target[pl.ds(below, HALO), HALO : HALO + along] = two_ref[...]
    for source, at in ((first_ref, 1 - odd_y), (second_ref, odd_y)):
        start = pl.multiple_of(at * (along + HALO), HALO)
        for k, row in enumerate((above, HALO, below)):
            target[pl.ds(row, HALO), pl.ds(start, HALO), :] = source[k * across : (k + 1) * across]


def conduct_kernel(sizes, place_ref, cells_ref, one_ref, two_ref, first_ref, second_ref, east_ref, north_ref, field):
    wide, tall, levels = field.shape
    across, along, _ = cells_ref.shape
    at_x, at_y = spot(place_ref, sizes)
    fill(at_x, at_y, field, cells_ref, one_ref, two_ref, first_ref, second_ref)
    edges = (at_x == 0, at_x == sizes[0] - 1, at_y == 0, at_y == sizes[1] - 1)

    @pl.when(edges[0])
    def _():
        field[:HALO] = jnp.zeros((HALO, tall, levels), f32)

    @pl.when(edges[1])
    def _():
        field[HALO + across :] = jnp.zeros((HALO, tall, levels), f32)

    @pl.when(edges[2])
    def _():
        field[:, :HALO] = jnp.zeros((wide, HALO, levels), f32)

    @pl.when(edges[3])
    def _():
        field[:, HALO + along :] = jnp.zeros((wide, HALO, levels), f32)

    def one(i, carry):
        here = COUPLING * field[i]
        after = field[jnp.minimum(i + 1, wide - 1)]
        east_ref[i] = here * after
        north_ref[i, : tall - 1] = here[: tall - 1] * field[i, 1:]
        north_ref[i, tall - 1 :] = jnp.zeros((1, levels), f32)
        return carry

    lax.fori_loop(0, wide, one, 0)


def select_kernel(send_ref, out_ref):
    slots, columns = out_ref.shape
    size = 128
    lane = lax.broadcasted_iota(jnp.int32, (size, size), 1).astype(f32)

    def one(index, carry):
        base = pl.multiple_of(index * size, size)
        wanted = jnp.broadcast_to(send_ref[:, pl.ds(base, size)].astype(f32), (size, size)).T
        for at in range(0, columns, size):
            hit = jnp.where(wanted == lane + at, 1.0, 0.0)
            out_ref[pl.ds(base, size), at : at + size] = hit.astype(bf16)
        return carry

    lax.fori_loop(0, slots // size, one, 0)


def smooth_kernel(sizes, place_ref, select_ref, cells_ref, one_ref, two_ref, first_ref, second_ref, east, north, *rest):
    *given, half_ref, full_ref, out_ref, sums_ref, field = rest
    across, along, levels = cells_ref.shape
    wide, tall = across + 2 * HALO, along + 2 * HALO
    fill(*spot(place_ref, sizes), field, cells_ref, one_ref, two_ref, first_ref, second_ref)

    def sweep(k):
        def row(i, carry):
            here, inward = carry
            after = field[i + 1]
            outward = east[i] * (after - here)
            above = north[i] * (pltpu.roll(here, tall - 1, 0) - here)
            field[i] = here + ((outward - inward) + (above - pltpu.roll(above, 1, 0)))
            return after, outward

        here = field[k]
        carry = (here, east[k - 1] * (here - field[k - 1]))
        for i in range(k, wide - k):
            carry = row(i, carry)

    def middle():
        return field[HALO : HALO + across, HALO : HALO + along]

    for k in range(1, PASSES + 1):
        sweep(k)
    half = middle()
    half_ref[...] = half
    if given:
        sums_ref[0] = jnp.sum((given[0][...] * half).reshape(-1, 8, levels), axis=0)
        sums_ref[1] = jnp.sum((half * half).reshape(-1, 8, levels), axis=0)
    else:
        sums_ref[0] = jnp.sum((half * half).reshape(-1, 8, levels), axis=0)
    for k in range(PASSES + 1, HALO + 1):
        sweep(k)
    full = middle()
    full_ref[...] = full
    columns = across * along
    pair = jnp.concatenate(halves(full.reshape(columns, levels)), axis=1)

    size = out_ref.shape[0] // 2
    for base in range(0, out_ref.shape[0], size):
        both = mm(select_ref[base : base + size, :], pair)
        out_ref[base : base + size, :] = both[:, :levels] + both[:, levels:]


def exact_sum(x, y):
    total = x + y
    part = total - x
    return total, (x - (total - part)) + (y - part)


def exact_product(x, y):
    def cut(value):
        scaled = 4097.0 * value
        high = scaled - (scaled - value)
        return high, value - high

    product = x * y
    (xh, xl), (yh, yl) = cut(x), cut(y)
    return product, ((xh * yh - product) + xh * yl + xl * yh) + xl * yl


def fraction(top, bottom):
    high = top[0] / bottom[0]
    product, rest = exact_product(high, bottom[0])
    return high, (((top[0] - product) - rest) + (top[1] - high * bottom[1])) / bottom[0]


def minus_product(x, y, z):
    product, rest = exact_product(y[0], z[0])
    return (x[0] - product) + ((x[1] - rest) - (y[0] * z[1] + y[1] * z[0]))


def finish_kernel(sums_ref, b_ref, sb_ref, p_ref, sp_ref, control_ref, increment_ref):
    total = sums_ref[...]
    error = jnp.zeros_like(total)
    while total.shape[0] > 1:
        half = total.shape[0] // 2
        total, more = exact_sum(total[:half], total[half:])
        error = (error[:half] + error[half:]) + more
    lane = lax.broadcasted_iota(jnp.int32, total.shape, 1)

    def pick(values, k):
        return jnp.sum(jnp.where(lane == k, values, 0.0), axis=1, keepdims=True)

    a, c, e, f = [(pick(total, k), pick(error, k)) for k in range(4)]
    slope, square, cube = fraction(c, a), fraction(e, a), fraction(f, a)
    first = 1.0 / (1.0 + slope[0])
    rest = minus_product(square, slope, slope)
    curved = rest + (minus_product(cube, slope, square) - slope[0] * rest)
    second = jnp.clip(rest / (curved - first * rest * rest), 0.0, 1.0)
    of_b = first + second * (first * first * rest + first * slope[0])
    of_p = -second * first
    control_ref[...] = of_b * b_ref[...] + of_p * p_ref[...]
    increment_ref[...] = of_b * sb_ref[...] + of_p * sp_ref[...]


def swap(cells, axis, odd):
    count = lax.axis_size(axis)
    pairs = [(i, (i + 1) % count) for i in range(odd, count, 2)]
    return lax.ppermute(cells, axis, pairs + [(j, i) for i, j in pairs])


def exchange(rows):
    return lax.all_to_all(rows, ("gx", "gy"), split_axis=0, concat_axis=0, tiled=True)


def params(mib):
    return pltpu.CompilerParams(vmem_limit_bytes=mib * MIB)


def cost(flops, size):
    return pl.CostEstimate(flops=flops, bytes_accessed=size, transcendentals=0)


def on_device(
    length_scale, innovation, observed_precision, profile_weight, stencil_weight, send_rows, stencil_rows, obs_count,
):
    across, along, levels = length_scale.shape
    owners, slot_count = send_rows.shape[1:]
    slots = owners * slot_count
    columns = across * along
    obs = innovation.shape[0]
    innovation = innovation.reshape(1, obs)
    precision = observed_precision.reshape(1, obs)
    sizes = tuple(lax.axis_size(axis) for axis in ("gx", "gy"))
    place = lax.axis_index(("gx", "gy")).astype(jnp.int32).reshape(1)

    whole = pl.BlockSpec(memory_space=pltpu.VMEM)
    scalar = pl.BlockSpec(memory_space=pltpu.SMEM)
    afar = pl.BlockSpec(memory_space=pltpu.HBM)
    slot_rows = jax.ShapeDtypeStruct((slots, levels), f32)
    tile = jax.ShapeDtypeStruct((across, along, levels), f32)
    strip = jax.ShapeDtypeStruct((across + 2 * HALO, HALO, levels), f32)
    grown = (across + 2 * HALO, along + 2 * HALO, levels)
    pair_scratch = pltpu.VMEM((2 * obs, 2 * levels), bf16)
    turned_scratch = pltpu.VMEM((2 * levels, slots), bf16)
    seen_scratch = pltpu.VMEM((1, obs), f32)

    def trade(rows):
        return exchange(rows.reshape(owners, slot_count, levels)).reshape(slots, levels)

    def strips(cells, one, two):
        return pl.pallas_call(
            functools.partial(strip_kernel, sizes),
            out_shape=(strip, strip),
            in_specs=[scalar] + [whole] * 3,
            out_specs=(whole, whole),
            compiler_params=params(2),
            name="strips",
        )(place, cells, one, two)

    def over_x(cells):
        return swap(cells, "gx", 0), swap(cells, "gx", 1)

    def over_y(first, second):
        return swap(first, "gy", 0), swap(second, "gy", 1)

    scale_x = over_x(length_scale)
    stencil_rows, place = lax.optimization_barrier((stencil_rows, place))
    turned = send_rows.transpose(0, 2, 1)
    given = (stencil_rows, stencil_weight, turned, innovation, precision, profile_weight)
    matrix, spread, send = pl.pallas_call(
        spread_first_kernel,
        out_shape=(
            jax.ShapeDtypeStruct((slots, 2 * obs), bf16),
            slot_rows,
            jax.ShapeDtypeStruct((1, slots), jnp.int32),
        ),
        in_specs=[scalar] + [afar] * 6,
        out_specs=(whole,) * 3,
        scratch_shapes=[
            *(pltpu.VMEM(x.shape, x.dtype) for x in given),
            pair_scratch,
            pltpu.SemaphoreType.DMA((6,)),
        ],
        compiler_params=params(14),
        cost_estimate=cost(8 << 30, 1 << 24),
        name="spread_first",
    )(obs_count, *(pltpu.with_memory_space_constraint(x, pltpu.HBM) for x in given))
    spread, *scale_x = lax.optimization_barrier((spread, *scale_x))
    arrived, send, *scale_x = lax.optimization_barrier((trade(spread), send, *scale_x))

    cells, placing = pl.pallas_call(
        place_first_kernel,
        out_shape=(jax.ShapeDtypeStruct((columns, levels), f32), jax.ShapeDtypeStruct((columns, slots), bf16)),
        in_specs=[whole, whole],
        out_specs=(whole, whole),
        scratch_shapes=[pltpu.VMEM((slots, 2 * levels), bf16)],
        compiler_params=params(8),
        name="place_first",
    )(send, arrived)
    selecting = pl.pallas_call(
        select_kernel,
        out_shape=jax.ShapeDtypeStruct((slots, columns), bf16),
        in_specs=[whole],
        out_specs=whole,
        compiler_params=params(2),
        cost_estimate=cost(1 << 28, 1 << 22),
        name="select",
    )(send)
    scale_y = over_y(*strips(length_scale, *scale_x))
    conductances = pl.pallas_call(
        functools.partial(conduct_kernel, sizes),
        out_shape=(jax.ShapeDtypeStruct(grown, f32),) * 2,
        in_specs=[scalar] + [whole] * 5,
        out_specs=(whole, whole),
        scratch_shapes=[pltpu.VMEM(grown, f32)],
        compiler_params=params(4),
        cost_estimate=cost(1 << 26, 1 << 22),
        name="conduct",
    )(place, length_scale, *scale_x, *scale_y)

    def smooth_twice(cells, given):
        cells = cells.reshape(across, along, levels)
        aside = over_x(cells)
        count = 1 + len(given)
        return pl.pallas_call(
            functools.partial(smooth_kernel, sizes),
            out_shape=(tile, tile, slot_rows, jax.ShapeDtypeStruct((count, 8, levels), f32)),
            in_specs=[scalar] + [whole] * (8 + len(given)),
            out_specs=(whole,) * 4,
            scratch_shapes=[pltpu.VMEM(grown, f32)],
            compiler_params=params(10),
            name="smooth",
        )(place, selecting, cells, *aside, *over_y(*strips(cells, *aside)), *conductances, *given)

    b, sb, outgoing, first_sums = smooth_twice(cells, ())

    spread, upright = pl.pallas_call(
        observe_adjoint_kernel,
        out_shape=(slot_rows, jax.ShapeDtypeStruct((levels, obs), f32)),
        in_specs=[scalar] + [whole] * 4,
        out_specs=(whole, whole),
        scratch_shapes=[turned_scratch, seen_scratch, pair_scratch],
        compiler_params=params(16),
        name="observe_adjoint",
    )(obs_count, trade(outgoing), precision, profile_weight, matrix)

    cells = pl.pallas_call(
        place_kernel,
        out_shape=jax.ShapeDtypeStruct((columns, levels), f32),
        in_specs=[whole, whole],
        out_specs=whole,
        scratch_shapes=[pltpu.VMEM((slots, 2 * levels), bf16)],
        compiler_params=params(8),
        name="place",
    )(placing, trade(spread))
    p, sp, outgoing, second_sums = smooth_twice(cells, (b,))

    sums = pl.pallas_call(
        observe_norm_kernel,
        out_shape=jax.ShapeDtypeStruct((owners, levels), f32),
        in_specs=[scalar] + [whole] * 6,
        out_specs=whole,
        scratch_shapes=[pltpu.VMEM((levels, slots), bf16), seen_scratch],
        compiler_params=params(14),
        name="observe_norm",
    )(obs_count, trade(outgoing), precision, upright, matrix, first_sums, second_sums)

    sums = exchange(sums.reshape(owners, 1, levels)).reshape(owners, levels)

    return pl.pallas_call(
        finish_kernel,
        out_shape=(
            jax.ShapeDtypeStruct((columns, levels), f32),
            jax.ShapeDtypeStruct((columns, levels), f32),
        ),
        in_specs=[whole] * 5,
        out_specs=(whole, whole),
        compiler_params=params(4),
        name="finish",
    )(sums, *(x.reshape(columns, levels) for x in (b, sb, p, sp)))


def solution(mesh):
    def run(*args):
        control, increment = on_device(*args)
        shape = args[0].shape
        return control.reshape(shape), increment.reshape(shape)

    return jax.shard_map(
        run,
        mesh=mesh,
        in_specs=(
            P("gx", "gy", None),
            P(("gx", "gy")),
            P(("gx", "gy")),
            P(("gx", "gy"), None),
            P(None, ("gx", "gy")),
            P(("gx", "gy"), None, None),
            P(None, ("gx", "gy")),
            P(("gx", "gy")),
        ),
        out_specs=(P("gx", "gy", None), P("gx", "gy", None)),
        check_vma=False,
    )
```

```python
import functools

import jax
import jax.numpy as jnp
from jax import lax
from jax.experimental import pallas as pl
from jax.experimental.pallas import tpu as pltpu
from jax.sharding import PartitionSpec as P


MIB = 1 << 20
COUPLING = 0.12
PASSES = 4
HALO = 2 * PASSES
CHUNK = 256
bf16 = jnp.bfloat16
f32 = jnp.float32


def mm(lhs, rhs):
    return jnp.dot(lhs, rhs, preferred_element_type=f32)


def halves(values):
    high = values.astype(bf16)
    return high, (values - high.astype(f32)).astype(bf16)


def live_precision(count_ref, precision_ref):
    place = lax.broadcasted_iota(jnp.int32, precision_ref.shape, 1)
    return jnp.where(place < count_ref[0], precision_ref[...], 0.0)


def merge_repeats(rows_ref, weights_ref):
    rows = [rows_ref[k : k + 1, :] for k in range(4)]
    weights = [weights_ref[k : k + 1, :] for k in range(4)]
    for k in range(1, 4):
        for j in range(k):
            same = rows[k] == rows[j]
            weights[j] = weights[j] + jnp.where(same, weights[k], 0.0)
            weights[k] = jnp.where(same, 0.0, weights[k])
    return rows, [halves(weight) for weight in weights]


def flatten_send(send_ref, out_ref):
    _, slot_count, owners = send_ref.shape
    lanes = 128
    group = lanes // slot_count
    wide = lax.broadcasted_iota(jnp.int32, (slot_count, lanes), 1)
    tall = lax.broadcasted_iota(jnp.int32, (slot_count, lanes), 0)
    again = jnp.where(lax.rem(wide, slot_count) == tall, 1.0, 0.0)
    repeated = jnp.dot(
        send_ref[0].astype(f32).T, again, precision=lax.Precision.HIGHEST, preferred_element_type=f32
    )
    owner = lax.broadcasted_iota(jnp.int32, (owners, lanes), 0)
    lane = lax.broadcasted_iota(jnp.int32, (owners, lanes), 1)
    kept = jnp.where(lax.div(lane, slot_count) == lax.rem(owner, group), repeated, 0.0)
    lines = jnp.sum(kept.reshape(owners // group, group, lanes), axis=1).astype(jnp.int32)
    for k in range(owners // group):
        out_ref[:, k * lanes : (k + 1) * lanes] = lines[k : k + 1]


def spread_first_kernel(
    count_ref, rows_hbm, weights_hbm, send_hbm, innovation_hbm, precision_hbm, profile_hbm,
    matrix_ref, out_ref, flat_ref,
    rows_ref, weights_ref, send_ref, innovation_ref, precision_ref, profile_ref, pair_ref, sems,
):
    moves = (
        (rows_hbm, rows_ref), (weights_hbm, weights_ref), (send_hbm, send_ref),
        (innovation_hbm, innovation_ref), (precision_hbm, precision_ref), (profile_hbm, profile_ref),
    )
    copies = [pltpu.make_async_copy(*move, sems.at[k]) for k, move in enumerate(moves)]
    for copy in copies:
        copy.start()
    for copy in copies[:5]:
        copy.wait()
    flatten_send(send_ref, flat_ref)
    rows, parts = merge_repeats(rows_ref, weights_ref)
    forcing = live_precision(count_ref, precision_ref) * innovation_ref[...]
    copies[5].wait()
    fill_pair(profile_ref, forcing, pair_ref)
    slots, obs, levels = matrix_ref.shape[0], rows_ref.shape[1], out_ref.shape[1]
    shape = (CHUNK, CHUNK)
    slot = lax.broadcasted_iota(jnp.int32, shape, 0).astype(f32).astype(bf16)

    def one(index, carry):
        base = pl.multiple_of(index * CHUNK, CHUNK)
        near = [(row - base).astype(f32).astype(bf16) for row in rows]
        for at in range(0, obs, CHUNK):
            high = jnp.zeros(shape, bf16)
            low = jnp.zeros(shape, bf16)
            for k in (3, 2, 1, 0):
                cut = slice(at, at + CHUNK)
                hit = jnp.broadcast_to(near[k][:, cut], shape) == slot
                high = jnp.where(hit, jnp.broadcast_to(parts[k][0][:, cut], shape), high)
                low = jnp.where(hit, jnp.broadcast_to(parts[k][1][:, cut], shape), low)
            matrix_ref[pl.ds(base, CHUNK), at : at + CHUNK] = high
            matrix_ref[pl.ds(base, CHUNK), obs + at : obs + at + CHUNK] = low
        both = mm(matrix_ref[pl.ds(base, CHUNK), :], pair_ref[...])
        out_ref[pl.ds(base, CHUNK), :] = both[:, :levels] + both[:, levels:]
        return carry

    lax.fori_loop(0, slots // CHUNK, one, 0)


def spread_rows(matrix_ref, pair_ref, out_ref):
    slots, levels = out_ref.shape
    size = slots // 2
    for base in range(0, slots, size):
        both = mm(matrix_ref[base : base + size, :], pair_ref[...])
        out_ref[base : base + size, :] = both[:, :levels] + both[:, levels:]


def fill_pair(profile_ref, forcing, pair_ref):
    obs, levels = profile_ref.shape
    for at in range(0, obs, levels):
        column = jnp.broadcast_to(forcing[:, at : at + levels], (levels, levels)).T
        high, low = halves(profile_ref[at : at + levels, :] * column)
        for base in (at, obs + at):
            pair_ref[base : base + levels, :levels] = high
            pair_ref[base : base + levels, levels:] = low


def observe(received_ref, matrix_ref, profile_ref, upright_ref, turned_ref, seen_ref):
    slots, levels = received_ref.shape
    obs = profile_ref.shape[0]
    for at in range(0, slots, levels):
        high, low = halves(received_ref[at : at + levels, :].T)
        turned_ref[:levels, at : at + levels] = high
        turned_ref[levels:, at : at + levels] = low
    size = obs // 2
    for base in range(0, obs, size):
        both = mm(turned_ref[...], matrix_ref[:, base : base + size])
        gathered = both[:levels] + both[levels:]
        gathered = gathered + mm(turned_ref[:levels], matrix_ref[:, obs + base : obs + base + size])
        upright = profile_ref[base : base + size, :].T
        upright_ref[:, base : base + size] = upright
        seen_ref[:, base : base + size] = jnp.sum(upright * gathered, axis=0, keepdims=True)


def observe_adjoint_kernel(
    count_ref, received_ref, precision_ref, profile_ref, matrix_ref, out_ref, upright_ref, turned_ref, seen_ref, pair_ref,
):
    observe(received_ref, matrix_ref, profile_ref, upright_ref, turned_ref, seen_ref)
    fill_pair(profile_ref, live_precision(count_ref, precision_ref) * seen_ref[...], pair_ref)
    spread_rows(matrix_ref, pair_ref, out_ref)


def observe_norm_kernel(
    count_ref, received_ref, precision_ref, upright_ref, matrix_ref, first_ref, second_ref,
    out_ref, turned_ref, seen_ref,
):
    slots, levels = received_ref.shape
    obs = upright_ref.shape[1]
    for at in range(0, slots, levels):
        turned_ref[:, at : at + levels] = received_ref[at : at + levels, :].T.astype(bf16)
    size = obs // 2
    for base in range(0, obs, size):
        gathered = mm(turned_ref[...], matrix_ref[:, base : base + size]) + mm(
            turned_ref[...], matrix_ref[:, obs + base : obs + base + size]
        )
        seen_ref[:, base : base + size] = jnp.sum(
            upright_ref[:, base : base + size] * gathered, axis=0, keepdims=True
        )
    seen = seen_ref[...]
    lane = lax.broadcasted_iota(jnp.int32, out_ref.shape, 1)
    parts = (first_ref[0], second_ref[0], second_ref[1], live_precision(count_ref, precision_ref) * seen * seen)
    row = jnp.zeros(out_ref.shape, f32)
    for k in range(4):
        row = jnp.where(lane == k, jnp.sum(parts[k]), row)
    out_ref[...] = row


def split_pair(arrived_ref, pair_ref):
    slots, levels = arrived_ref.shape
    for base in range(0, slots, CHUNK):
        high, low = halves(arrived_ref[base : base + CHUNK, :])
        pair_ref[base : base + CHUNK, :levels] = high
        pair_ref[base : base + CHUNK, levels:] = low


def place_first_kernel(send_ref, arrived_ref, out_ref, matrix_ref, pair_ref):
    slots, levels = arrived_ref.shape
    split_pair(arrived_ref, pair_ref)
    size = 128
    shape = (size, CHUNK)
    column = lax.broadcasted_iota(jnp.int32, shape, 0).astype(f32).astype(bf16)
    one, zero = jnp.ones(shape, bf16), jnp.zeros(shape, bf16)
    for base in range(0, out_ref.shape[0], size):
        near = (send_ref[...] - base).astype(f32).astype(bf16)
        for at in range(0, slots, CHUNK):
            hit = jnp.broadcast_to(near[:, at : at + CHUNK], shape) == column
            matrix_ref[base : base + size, at : at + CHUNK] = jnp.where(hit, one, zero)
    both = mm(matrix_ref[...], pair_ref[...])
    out_ref[...] = both[:, :levels] + both[:, levels:]


def place_kernel(matrix_ref, arrived_ref, out_ref, pair_ref):
    levels = arrived_ref.shape[1]
    split_pair(arrived_ref, pair_ref)
    both = mm(matrix_ref[...], pair_ref[...])
    out_ref[...] = both[:, :levels] + both[:, levels:]


def spot(place_ref, sizes):
    return lax.div(place_ref[0], sizes[1]), lax.rem(place_ref[0], sizes[1])


def strip_kernel(sizes, place_ref, cells_ref, one_ref, two_ref, first_ref, second_ref):
    across, along, _ = cells_ref.shape
    odd = lax.rem(spot(place_ref, sizes)[1], 2)
    head_or_tail = pl.multiple_of((1 - odd) * (along - HALO), HALO)
    tail_or_head = pl.multiple_of(odd * (along - HALO), HALO)
    for target, at in ((first_ref, head_or_tail), (second_ref, tail_or_head)):
        for k, source in enumerate((one_ref, cells_ref, two_ref)):
            target[k * across : (k + 1) * across] = source[:, pl.ds(at, HALO), :]


def fill(at_x, at_y, target, cells_ref, one_ref, two_ref, first_ref, second_ref):
    across, along, _ = cells_ref.shape
    odd_x, odd_y = lax.rem(at_x, 2), lax.rem(at_y, 2)
    above = (1 - odd_x) * (across + HALO)
    below = odd_x * (across + HALO)
    target[HALO : HALO + across, HALO : HALO + along] = cells_ref[...]
    target[pl.ds(above, HALO), HALO : HALO + along] = one_ref[...]
    target[pl.ds(below, HALO), HALO : HALO + along] = two_ref[...]
    for source, at in ((first_ref, 1 - odd_y), (second_ref, odd_y)):
        start = pl.multiple_of(at * (along + HALO), HALO)
        for k, row in enumerate((above, HALO, below)):
            target[pl.ds(row, HALO), pl.ds(start, HALO), :] = source[k * across : (k + 1) * across]


def conduct_kernel(sizes, place_ref, cells_ref, one_ref, two_ref, first_ref, second_ref, east_ref, north_ref, field):
    wide, tall, levels = field.shape
    across, along, _ = cells_ref.shape
    at_x, at_y = spot(place_ref, sizes)
    fill(at_x, at_y, field, cells_ref, one_ref, two_ref, first_ref, second_ref)
    edges = (at_x == 0, at_x == sizes[0] - 1, at_y == 0, at_y == sizes[1] - 1)

    @pl.when(edges[0])
    def _():
        field[:HALO] = jnp.zeros((HALO, tall, levels), f32)

    @pl.when(edges[1])
    def _():
        field[HALO + across :] = jnp.zeros((HALO, tall, levels), f32)

    @pl.when(edges[2])
    def _():
        field[:, :HALO] = jnp.zeros((wide, HALO, levels), f32)

    @pl.when(edges[3])
    def _():
        field[:, HALO + along :] = jnp.zeros((wide, HALO, levels), f32)

    def one(i, carry):
        here = COUPLING * field[i]
        after = field[jnp.minimum(i + 1, wide - 1)]
        east_ref[i] = here * after
        north_ref[i, : tall - 1] = here[: tall - 1] * field[i, 1:]
        north_ref[i, tall - 1 :] = jnp.zeros((1, levels), f32)
        return carry

    lax.fori_loop(0, wide, one, 0)


def select_kernel(send_ref, out_ref):
    slots, columns = out_ref.shape
    size = 128
    lane = lax.broadcasted_iota(jnp.int32, (size, size), 1).astype(f32)

    def one(index, carry):
        base = pl.multiple_of(index * size, size)
        wanted = jnp.broadcast_to(send_ref[:, pl.ds(base, size)].astype(f32), (size, size)).T
        for at in range(0, columns, size):
            hit = jnp.where(wanted == lane + at, 1.0, 0.0)
            out_ref[pl.ds(base, size), at : at + size] = hit.astype(bf16)
        return carry

    lax.fori_loop(0, slots // size, one, 0)


def smooth_kernel(sizes, place_ref, select_ref, cells_ref, one_ref, two_ref, first_ref, second_ref, east, north, *rest):
    *given, half_ref, full_ref, out_ref, sums_ref, field = rest
    across, along, levels = cells_ref.shape
    wide, tall = across + 2 * HALO, along + 2 * HALO
    fill(*spot(place_ref, sizes), field, cells_ref, one_ref, two_ref, first_ref, second_ref)

    def sweep(k):
        def row(i, carry):
            here, inward = carry
            after = field[i + 1]
            outward = east[i] * (after - here)
            above = north[i] * (pltpu.roll(here, tall - 1, 0) - here)
            field[i] = here + ((outward - inward) + (above - pltpu.roll(above, 1, 0)))
            return after, outward

        here = field[k]
        carry = (here, east[k - 1] * (here - field[k - 1]))
        for i in range(k, wide - k):
            carry = row(i, carry)

    def middle():
        return field[HALO : HALO + across, HALO : HALO + along]

    for k in range(1, PASSES + 1):
        sweep(k)
    half = middle()
    half_ref[...] = half
    if given:
        sums_ref[0] = jnp.sum((given[0][...] * half).reshape(-1, 8, levels), axis=0)
        sums_ref[1] = jnp.sum((half * half).reshape(-1, 8, levels), axis=0)
    else:
        sums_ref[0] = jnp.sum((half * half).reshape(-1, 8, levels), axis=0)
    for k in range(PASSES + 1, HALO + 1):
        sweep(k)
    full = middle()
    full_ref[...] = full
    columns = across * along
    size = out_ref.shape[0] // 2
    high, low = halves(full.reshape(columns, levels))
    pair = high if given else jnp.concatenate((high, low), axis=1)
    for base in range(0, out_ref.shape[0], size):
        both = mm(select_ref[base : base + size, :], pair)
        out_ref[base : base + size, :] = both if given else both[:, :levels] + both[:, levels:]


def exact_sum(x, y):
    total = x + y
    part = total - x
    return total, (x - (total - part)) + (y - part)


def exact_product(x, y):
    def cut(value):
        scaled = 4097.0 * value
        high = scaled - (scaled - value)
        return high, value - high

    product = x * y
    (xh, xl), (yh, yl) = cut(x), cut(y)
    return product, ((xh * yh - product) + xh * yl + xl * yh) + xl * yl


def fraction(top, bottom):
    high = top[0] / bottom[0]
    product, rest = exact_product(high, bottom[0])
    return high, (((top[0] - product) - rest) + (top[1] - high * bottom[1])) / bottom[0]


def minus_product(x, y, z):
    product, rest = exact_product(y[0], z[0])
    return (x[0] - product) + ((x[1] - rest) - (y[0] * z[1] + y[1] * z[0]))


def finish_kernel(sums_ref, b_ref, sb_ref, p_ref, sp_ref, control_ref, increment_ref):
    total = sums_ref[...]
    error = jnp.zeros_like(total)
    while total.shape[0] > 1:
        half = total.shape[0] // 2
        total, more = exact_sum(total[:half], total[half:])
        error = (error[:half] + error[half:]) + more
    lane = lax.broadcasted_iota(jnp.int32, total.shape, 1)

    def pick(values, k):
        return jnp.sum(jnp.where(lane == k, values, 0.0), axis=1, keepdims=True)

    a, c, e, f = [(pick(total, k), pick(error, k)) for k in range(4)]
    slope, square, cube = fraction(c, a), fraction(e, a), fraction(f, a)
    first = 1.0 / (1.0 + slope[0])
    rest = minus_product(square, slope, slope)
    curved = rest + (minus_product(cube, slope, square) - slope[0] * rest)
    second = jnp.clip(rest / (curved - first * rest * rest), 0.0, 1.0)
    of_b = first + second * (first * first * rest + first * slope[0])
    of_p = -second * first
    control_ref[...] = of_b * b_ref[...] + of_p * p_ref[...]
    increment_ref[...] = of_b * sb_ref[...] + of_p * sp_ref[...]


def swap(cells, axis, odd):
    count = lax.axis_size(axis)
    pairs = [(i, (i + 1) % count) for i in range(odd, count, 2)]
    return lax.ppermute(cells, axis, pairs + [(j, i) for i, j in pairs])


def exchange(rows):
    return lax.all_to_all(rows, ("gx", "gy"), split_axis=0, concat_axis=0, tiled=True)


def params(mib):
    return pltpu.CompilerParams(vmem_limit_bytes=mib * MIB)


def cost(flops, size):
    return pl.CostEstimate(flops=flops, bytes_accessed=size, transcendentals=0)


def on_device(
    length_scale, innovation, observed_precision, profile_weight, stencil_weight, send_rows, stencil_rows, obs_count,
):
    across, along, levels = length_scale.shape
    owners, slot_count = send_rows.shape[1:]
    slots = owners * slot_count
    columns = across * along
    obs = innovation.shape[0]
    innovation = innovation.reshape(1, obs)
    precision = observed_precision.reshape(1, obs)
    sizes = tuple(lax.axis_size(axis) for axis in ("gx", "gy"))
    place = lax.axis_index(("gx", "gy")).astype(jnp.int32).reshape(1)

    whole = pl.BlockSpec(memory_space=pltpu.VMEM)
    scalar = pl.BlockSpec(memory_space=pltpu.SMEM)
    afar = pl.BlockSpec(memory_space=pltpu.HBM)
    slot_rows = jax.ShapeDtypeStruct((slots, levels), f32)
    tile = jax.ShapeDtypeStruct((across, along, levels), f32)
    strip = jax.ShapeDtypeStruct((across + 2 * HALO, HALO, levels), f32)
    grown = (across + 2 * HALO, along + 2 * HALO, levels)
    pair_scratch = pltpu.VMEM((2 * obs, 2 * levels), bf16)
    turned_scratch = pltpu.VMEM((2 * levels, slots), bf16)
    seen_scratch = pltpu.VMEM((1, obs), f32)

    def trade(rows):
        return exchange(rows.reshape(owners, slot_count, levels)).reshape(slots, levels)

    def strips(cells, one, two):
        return pl.pallas_call(
            functools.partial(strip_kernel, sizes),
            out_shape=(strip, strip),
            in_specs=[scalar] + [whole] * 3,
            out_specs=(whole, whole),
            compiler_params=params(2),
            name="strips",
        )(place, cells, one, two)

    def over_x(cells):
        return swap(cells, "gx", 0), swap(cells, "gx", 1)

    def over_y(first, second):
        return swap(first, "gy", 0), swap(second, "gy", 1)

    scale_x = over_x(length_scale)
    stencil_rows, place = lax.optimization_barrier((stencil_rows, place))
    turned = send_rows.transpose(0, 2, 1)
    given = (stencil_rows, stencil_weight, turned, innovation, precision, profile_weight)
    matrix, spread, send = pl.pallas_call(
        spread_first_kernel,
        out_shape=(
            jax.ShapeDtypeStruct((slots, 2 * obs), bf16),
            slot_rows,
            jax.ShapeDtypeStruct((1, slots), jnp.int32),
        ),
        in_specs=[scalar] + [afar] * 6,
        out_specs=(whole,) * 3,
        scratch_shapes=[
            *(pltpu.VMEM(x.shape, x.dtype) for x in given),
            pair_scratch,
            pltpu.SemaphoreType.DMA((6,)),
        ],
        compiler_params=params(14),
        cost_estimate=cost(8 << 30, 1 << 24),
        name="spread_first",
    )(obs_count, *(pltpu.with_memory_space_constraint(x, pltpu.HBM) for x in given))
    spread, *scale_x = lax.optimization_barrier((spread, *scale_x))
    arrived, send, *scale_x = lax.optimization_barrier((trade(spread), send, *scale_x))

    cells, placing = pl.pallas_call(
        place_first_kernel,
        out_shape=(jax.ShapeDtypeStruct((columns, levels), f32), jax.ShapeDtypeStruct((columns, slots), bf16)),
        in_specs=[whole, whole],
        out_specs=(whole, whole),
        scratch_shapes=[pltpu.VMEM((slots, 2 * levels), bf16)],
        compiler_params=params(8),
        name="place_first",
    )(send, arrived)
    selecting = pl.pallas_call(
        select_kernel,
        out_shape=jax.ShapeDtypeStruct((slots, columns), bf16),
        in_specs=[whole],
        out_specs=whole,
        compiler_params=params(2),
        cost_estimate=cost(1 << 28, 1 << 22),
        name="select",
    )(send)
    scale_y = over_y(*strips(length_scale, *scale_x))
    conductances = pl.pallas_call(
        functools.partial(conduct_kernel, sizes),
        out_shape=(jax.ShapeDtypeStruct(grown, f32),) * 2,
        in_specs=[scalar] + [whole] * 5,
        out_specs=(whole, whole),
        scratch_shapes=[pltpu.VMEM(grown, f32)],
        compiler_params=params(4),
        cost_estimate=cost(1 << 26, 1 << 22),
        name="conduct",
    )(place, length_scale, *scale_x, *scale_y)

    def smooth_twice(cells, given):
        cells = cells.reshape(across, along, levels)
        aside = over_x(cells)
        count = 1 + len(given)
        return pl.pallas_call(
            functools.partial(smooth_kernel, sizes),
            out_shape=(tile, tile, slot_rows, jax.ShapeDtypeStruct((count, 8, levels), f32)),
            in_specs=[scalar] + [whole] * (8 + len(given)),
            out_specs=(whole,) * 4,
            scratch_shapes=[pltpu.VMEM(grown, f32)],
            compiler_params=params(10),
            name="smooth",
        )(place, selecting, cells, *aside, *over_y(*strips(cells, *aside)), *conductances, *given)

    b, sb, outgoing, first_sums = smooth_twice(cells, ())

    spread, upright = pl.pallas_call(
        observe_adjoint_kernel,
        out_shape=(slot_rows, jax.ShapeDtypeStruct((levels, obs), f32)),
        in_specs=[scalar] + [whole] * 4,
        out_specs=(whole, whole),
        scratch_shapes=[turned_scratch, seen_scratch, pair_scratch],
        compiler_params=params(16),
        name="observe_adjoint",
    )(obs_count, trade(outgoing), precision, profile_weight, matrix)

    cells = pl.pallas_call(
        place_kernel,
        out_shape=jax.ShapeDtypeStruct((columns, levels), f32),
        in_specs=[whole, whole],
        out_specs=whole,
        scratch_shapes=[pltpu.VMEM((slots, 2 * levels), bf16)],
        compiler_params=params(8),
        name="place",
    )(placing, trade(spread))
    p, sp, outgoing, second_sums = smooth_twice(cells, (b,))

    sums = pl.pallas_call(
        observe_norm_kernel,
        out_shape=jax.ShapeDtypeStruct((owners, levels), f32),
        in_specs=[scalar] + [whole] * 6,
        out_specs=whole,
        scratch_shapes=[pltpu.VMEM((levels, slots), bf16), seen_scratch],
        compiler_params=params(14),
        name="observe_norm",
    )(obs_count, trade(outgoing), precision, upright, matrix, first_sums, second_sums)

    sums = exchange(sums.reshape(owners, 1, levels)).reshape(owners, levels)

    return pl.pallas_call(
        finish_kernel,
        out_shape=(
            jax.ShapeDtypeStruct((columns, levels), f32),
            jax.ShapeDtypeStruct((columns, levels), f32),
        ),
        in_specs=[whole] * 5,
        out_specs=(whole, whole),
        compiler_params=params(4),
        name="finish",
    )(sums, *(x.reshape(columns, levels) for x in (b, sb, p, sp)))


def solution(mesh):
    def run(*args):
        control, increment = on_device(*args)
        shape = args[0].shape
        return control.reshape(shape), increment.reshape(shape)

    return jax.shard_map(
        run,
        mesh=mesh,
        in_specs=(
            P("gx", "gy", None),
            P(("gx", "gy")),
            P(("gx", "gy")),
            P(("gx", "gy"), None),
            P(None, ("gx", "gy")),
            P(("gx", "gy"), None, None),
            P(None, ("gx", "gy")),
            P(("gx", "gy")),
        ),
        out_specs=(P("gx", "gy", None), P("gx", "gy", None)),
        check_vma=False,
    )
```
